32 devices in a mesh: league: 4 (over x, core), env: 8 (over z, y).
Axes of the slice: x: 2, y: 2, z: 4, core: 2. Of those that a mesh axis runs over, the one named last changes fastest.
Arguments:
- obs_own: bfloat16 [4, 2, 128, 16, 2048], P('league', None, 'env'), may hold values from -6 to 6
- obs_opp: bfloat16 [4, 2, 128, 16, 2048], P('league', None, 'env'), may hold values from -6 to 6
- actions: int32 [4, 2, 2, 128, 16], P('league', None, None, 'env'), may hold values from 0 to 255
- opponent_picks: int32 [4, 2], P('league'), may hold values from 0 to 3
- policy_weight: bfloat16 [4, 2048, 2048], P('league', 'env'), may hold values from -0.125 to 0.125
- policy_gain: bfloat16 [4, 2048], P('league'), may hold values from 0.25 to 1.75
- action_table: bfloat16 [256, 2048], replicated, may hold values from -6 to 6
- value_gain: bfloat16 [2048], replicated, may hold values from 0.25 to 1.75
- value_up: bfloat16 [2048, 1024], replicated, may hold values from -0.125 to 0.125
- value_out: bfloat16 [1024], replicated, may hold values from -0.1875 to 0.1875
Outputs:
- learner_rows: bfloat16 [4, 2, 16, 2048, 128], P('league', None, None, 'env')
- values: float32 [4, 2, 128, 16], P('league', None, 'env')
The draws below stay inside these ranges and needn't reach their ends.
All inputs are finite; a program needn't handle non-finite values.
Results may differ from the reference program's by a relative error of at most 0.0054.
Values may be sent and summed in bfloat16 or wider, within the bound.
A program may use at most 128 MiB of HBM per device.

```python
import jax
import jax.numpy as jnp
from jax import lax

D = 2048
VH = 1024
ACTIONS = 256
STEPS = 16
ROUNDS = 2
GROUPS = 4
ENVS = 128


def with_ends(array, rng, low, high):
    place = [jax.random.randint(jax.random.fold_in(rng, axis), (), 0, length) for axis, length in enumerate(array.shape)]
    widest = array.shape.index(max(array.shape))
    beside = place[:widest] + [(place[widest] + 1) % array.shape[widest]] + place[widest + 1:]
    return array.at[tuple(place)].set(low).at[tuple(beside)].set(high)


def steps_of(key, extent, shards, low, top_value):
    def one(dim, blocks):
        steps = jax.random.uniform(jax.random.fold_in(jax.random.fold_in(key, 6), dim), (blocks,), jnp.float32, low / len(shards), top_value / len(shards))
        return jnp.repeat(jnp.exp(steps), extent[dim] // blocks).reshape((-1,) + (1,) * (len(extent) - dim - 1))

    loudness = one(*shards[0])
    for cut in shards[1:]:
        loudness = loudness * one(*cut)
    return loudness


def centred(own_key, extent, width, most, pieces=(), held_as=jnp.bfloat16):
    values = jax.random.normal(own_key, extent, jnp.float32) * width
    if len(pieces) > 0:
        values = steps_of(own_key, extent, pieces, -0.22, 0.18) * values
    return jnp.clip(values, min=-most, max=most).astype(held_as)


def setup_inputs(seed: int = 0) -> dict:
    arg_keys = jax.random.split(jax.random.key(seed), 11)
    obs_own = centred(arg_keys[0], (GROUPS, ROUNDS, ENVS, STEPS, D), 1.0, 6.0, ((0, 4), (2, 8)))
    obs_opp = centred(arg_keys[1], (GROUPS, ROUNDS, ENVS, STEPS, D), 1.0, 6.0, ((0, 4), (2, 8)))
    actions = with_ends(jax.random.randint(arg_keys[2], (GROUPS, 2, ROUNDS, ENVS, STEPS), 0, ACTIONS), jax.random.fold_in(arg_keys[2], 1), 0, ACTIONS - 1).astype(jnp.int32)
    opponent_picks = with_ends(jax.random.randint(arg_keys[3], (GROUPS, ROUNDS), 0, GROUPS), jax.random.fold_in(arg_keys[3], 1), 0, GROUPS - 1).astype(jnp.int32)
    policy_weight = centred(arg_keys[4], (GROUPS, D, D), D ** -0.5, 0.125, ((0, 4), (1, 8)))
    policy_gain = jnp.clip(1.0 + 0.15 * jax.random.normal(arg_keys[5], (GROUPS, D), jnp.float32), 0.25, 1.75).astype(jnp.bfloat16)
    action_table = centred(arg_keys[6], (ACTIONS, D), 1.0, 6.0)
    value_gain = jnp.clip(1.0 + 0.15 * jax.random.normal(arg_keys[7], (D,), jnp.float32), 0.25, 1.75).astype(jnp.bfloat16)
    value_up = centred(arg_keys[8], (D, VH), D ** -0.5, 0.125)
    value_out = centred(arg_keys[9], (VH,), VH ** -0.5, 0.1875)
    return {"obs_own": obs_own, "obs_opp": obs_opp, "actions": actions, "opponent_picks": opponent_picks, "policy_weight": policy_weight, "policy_gain": policy_gain, "action_table": action_table, "value_gain": value_gain, "value_up": value_up, "value_out": value_out}


def rms_norm(inputs, gain):
    scale = lax.rsqrt(lax.optimization_barrier(jnp.mean(inputs * inputs, axis=-1, keepdims=True)) + 1e-05)
    return inputs * scale * gain.astype(jnp.float32)

def policy(inputs, weight, gain):
    values_f = inputs.astype(jnp.float32)
    normed = rms_norm(values_f, gain).astype(jnp.bfloat16)
    return values_f + jnp.dot(normed, weight, preferred_element_type=jnp.float32)

def reference(obs_own, obs_opp, actions, opponent_picks, policy_weight, policy_gain, action_table, value_gain, value_up, value_out):
    row_count = ENVS * STEPS

    def one_group(group_index):
        traj_list = []
        value_list = []
        for round_index in range(ROUNDS):
            opp_index = opponent_picks[group_index, round_index]
            own_state = policy(obs_own[group_index, round_index].reshape(row_count, D), policy_weight[group_index], policy_gain[group_index])
            opp_state = policy(obs_opp[group_index, round_index].reshape(row_count, D), policy_weight[opp_index], policy_gain[opp_index])
            own_ids = actions[group_index, 0, round_index].reshape(row_count)
            opp_ids = actions[group_index, 1, round_index].reshape(row_count)
            action_sum = action_table[own_ids].astype(jnp.float32) + action_table[opp_ids].astype(jnp.float32)
            joint_sum = own_state + opp_state + action_sum
            joint_row = rms_norm(joint_sum, value_gain).astype(jnp.bfloat16)
            value_hidden = jax.nn.silu(jnp.dot(joint_row, value_up, preferred_element_type=jnp.float32)).astype(jnp.bfloat16)
            value_est = jnp.dot(value_hidden, value_out, preferred_element_type=jnp.float32)
            value_list.append(value_est.reshape(ENVS, STEPS))
            traj_list.append(joint_row.reshape(ENVS, STEPS, D).transpose(1, 2, 0))
        return (jnp.stack(traj_list), jnp.stack(value_list))
    learner_rows, values = lax.map(one_group, jnp.arange(GROUPS, dtype=jnp.int32))
    return (learner_rows, values)
```

```python
import functools

import jax
import jax.numpy as jnp
from jax import lax
from jax.experimental import pallas as pl
from jax.experimental.pallas import tpu as pltpu
from jax.sharding import PartitionSpec as P

F32 = jnp.float32
BF16 = jnp.bfloat16
BLOCKS = 4
LINE = 4
PAIR = 2
MIB = 1 << 20
OWN, ME, SIB, ACROSS, DIAG = range(5)
MESH = pl.DeviceIdType.MESH


def rms_norm(inputs, gain):
    scale = lax.rsqrt(jnp.mean(inputs * inputs, axis=-1, keepdims=True) + 1e-05)
    return inputs * scale * gain.astype(jnp.float32)


def local(
    obs_own,
    obs_opp,
    actions,
    opponent_picks,
    policy_weight,
    policy_gain,
    action_table,
    value_gain,
    value_up,
    value_out,
):
    round_count = obs_own.shape[1]
    env_count = obs_own.shape[2]
    step_count = obs_own.shape[3]
    model_width = obs_own.shape[4]
    row_count = env_count * step_count
    weight_shard = policy_weight[0]
    own_gain = policy_gain[0]
    group_count = lax.axis_size("league")
    my_group = lax.axis_index("league")
    own_inputs = obs_own[0].reshape(round_count * row_count, model_width).astype(jnp.float32)
    own_normed = rms_norm(own_inputs, own_gain).astype(jnp.bfloat16)
    own_whole = lax.all_gather(weight_shard, "env", axis=0, tiled=True)
    own_state = own_inputs + jnp.dot(own_normed, own_whole, preferred_element_type=jnp.float32)
    every_pick = lax.all_gather(opponent_picks, "league", axis=0, tiled=True)
    action_range = jnp.arange(action_table.shape[0], dtype=jnp.int32)
    traj_list = []
    value_list = []
    for round_index in range(round_count):
        opp_raw = obs_opp[0, round_index].reshape(row_count, model_width)
        opp_inputs = opp_raw.astype(jnp.float32)
        all_rows = lax.all_gather(opp_raw, "league", axis=0, tiled=True)
        all_normed = rms_norm(all_rows.astype(jnp.float32), own_gain).astype(jnp.bfloat16)
        products = jnp.dot(all_normed, own_whole, preferred_element_type=jnp.float32)
        served = (every_pick[:, round_index] == my_group).astype(jnp.float32)
        products = (
            products.reshape(group_count, row_count, model_width) * served[:, None, None]
        ).astype(jnp.bfloat16)
        answers = lax.all_to_all(products, "league", split_axis=0, concat_axis=0, tiled=True)
        opp_state = opp_inputs + jnp.sum(answers.astype(jnp.float32), axis=0)
        own_ids = actions[0, 0, round_index].reshape(row_count)
        opp_ids = actions[0, 1, round_index].reshape(row_count)
        onehot = (own_ids[:, None] == action_range[None, :]).astype(jnp.bfloat16) + (
            opp_ids[:, None] == action_range[None, :]
        ).astype(jnp.bfloat16)
        action_sum = jnp.dot(onehot, action_table, preferred_element_type=jnp.float32)
        round_state = lax.dynamic_slice_in_dim(own_state, round_index * row_count, row_count, 0)
        joint_sum = round_state + opp_state + action_sum
        joint_row = rms_norm(joint_sum, value_gain).astype(jnp.bfloat16)
        value_hidden = jax.nn.silu(
            jnp.dot(joint_row, value_up, preferred_element_type=jnp.float32)
        ).astype(jnp.bfloat16)
        value_est = jnp.dot(value_hidden, value_out, preferred_element_type=jnp.float32)
        value_list.append(value_est.reshape(env_count, step_count))
        time_block = joint_row.reshape(env_count, step_count, model_width).transpose(1, 2, 0)
        traj_list.append(lax.all_to_all(time_block, "env", split_axis=1, concat_axis=2, tiled=True))
    learner_rows = jnp.stack(traj_list)
    values = jnp.stack(value_list)
    return (learner_rows[None], values[None])


def dest(b, j):
    return jnp.where(b < 2, j + LINE * (j // 2), PAIR + j)


def window_kernel(
    w_hbm, own_hbm, opp_hbm, acts_ref, picks_ref, gain_ref, vgain_ref, vout_ref, table_hbm, up_hbm,
    out_ref, scale_ref, val_ref,
    wbuf, rows, own_ref, opp_ref, table, up, tag, picks_all, onehot, order,
    to_sib, from_sib, to_x, from_x, part, ssq, hid, jrow, jsend, arecv, sc_send, sc_recv,
    l_sem, b_sem, w_send, w_recv, o_send, o_recv, p_send, p_recv, s_send, s_recv, x_send, x_recv,
    a_send, a_recv, c_send, c_recv,
):
    blocks, env, depth, width = wbuf.shape
    rounds, count, model = own_ref.shape
    pieces, steps, envs, lane = jsend.shape[2:]
    share = model // env
    league_me = lax.axis_index("league")
    me = lax.axis_index("env")
    x, core = league_me // 2, league_me % 2
    z, y = me // PAIR, me % PAIR
    sib = x * 2 + (1 - core)
    across = (1 - x) * 2 + core
    diag = (1 - x) * 2 + (1 - core)
    y_peer = z * PAIR + (1 - y)

    barrier = pltpu.get_barrier_semaphore()
    for group in (sib, across, diag):
        pl.semaphore_signal(barrier, inc=1, device_id=(group, me), device_id_type=MESH)
    for d in range(1, env):
        pl.semaphore_signal(barrier, inc=1, device_id=(league_me, (me + d) % env), device_id_type=MESH)

    def piece_copy(kind, b, j):
        start = pl.multiple_of(dest(b, j) * share + (b % 2) * lane, lane)
        cols = pl.ds(j * lane, lane)
        if kind == 0:
            src, dst = w_hbm.at[:, pl.ds(start, lane)], wbuf.at[b, me, :, cols]
        elif kind == 1:
            src, dst = table_hbm.at[:, pl.ds(start, lane)], table.at[b, :, cols]
        else:
            src, dst = up_hbm.at[pl.ds(start, lane)], up.at[b, cols]
        return pltpu.make_async_copy(src, dst, b_sem.at[kind, b, j])

    own_in = pltpu.make_async_copy(own_hbm, own_ref, l_sem.at[0])
    opp_in = pltpu.make_async_copy(opp_hbm, opp_ref, l_sem.at[1])
    for b in range(blocks):
        for j in range(pieces):
            piece_copy(0, b, j).start()
    own_in.start()
    opp_in.start()
    for kind in (1, 2):
        for b in range(blocks):
            for j in range(pieces):
                piece_copy(kind, b, j).start()

    def remote(src, dst, send, recv, group, place):
        return pltpu.make_async_remote_copy(
            src_ref=src, dst_ref=dst, send_sem=send, recv_sem=recv,
            device_id=(group, place), device_id_type=MESH,
        )

    def w_copy(b, line, way, place):
        slot = line * PAIR + y
        return remote(
            wbuf.at[b, slot], wbuf.at[b, slot], w_send.at[b, line, way], w_recv.at[b, slot], league_me, place
        )

    def to_right(b, line):
        return w_copy(b, line, 0, me + PAIR)

    def to_left(b, line):
        return w_copy(b, line, 1, me - PAIR)

    def to_y(b, line):
        return w_copy(b, line, 2, y_peer)

    def w_wait(b, slot):
        remote(
            wbuf.at[b, slot], wbuf.at[b, slot], w_send.at[b, 0, 2], w_recv.at[b, slot], league_me, y_peer
        ).wait_recv()

    def own_sends(b):
        @pl.when(z < LINE - 1)
        def _():
            to_right(b, z).start()

        @pl.when(z > 0)
        def _():
            to_left(b, z).start()

        to_y(b, z).start()

    def hop(k):
        b, h = k // (LINE - 1), k % (LINE - 1) + 1
        low, high = z - h, z + h

        @pl.when(low >= 0)
        def _():
            w_wait(b, low * PAIR + y)

            @pl.when(z < LINE - 1)
            def _():
                to_right(b, low).start()

            to_y(b, low).start()

        @pl.when(high < LINE)
        def _():
            w_wait(b, high * PAIR + y)

            @pl.when(z > 0)
            def _():
                to_left(b, high).start()

            to_y(b, high).start()

        @pl.when(jnp.logical_and(h == 2, b < blocks - 1))
        def _():
            own_sends(b + 1)

    def finish_w_sends(b):
        for line in range(LINE):
            @pl.when(jnp.logical_and(line <= z, z < LINE - 1))
            def _():
                to_right(b, line).wait_send()

            @pl.when(jnp.logical_and(line >= z, z > 0))
            def _():
                to_left(b, line).wait_send()

            to_y(b, line).wait_send()

    def o_copy(r, way):
        if way == 0:
            src, dst, group = opp_hbm.at[r], rows.at[r, ACROSS], across
        elif way == 1:
            src, dst, group = opp_hbm.at[r], rows.at[r, SIB], sib
        else:
            src, dst, group = rows.at[r, ACROSS], rows.at[r, DIAG], sib
        return remote(src, dst, o_send.at[way, r], o_recv.at[way, r], group, me)

    pick_copies = [
        remote(tag, picks_all.at[slot], p_send.at[slot], p_recv.at[slot], group, me)
        for slot, group in ((SIB, sib), (ACROSS, across), (DIAG, diag))
    ]

    def norm(src, dst, tile=64):
        def step(i, _):
            at = pl.ds(pl.multiple_of(i * tile, tile), tile)
            v = src[at, :].astype(F32)
            scale = lax.rsqrt(jnp.mean(v * v, axis=-1, keepdims=True) + 1e-05)
            dst[at, :] = (v * scale * gain_ref[...].astype(F32)).astype(BF16)
            return 0

        lax.fori_loop(0, count // tile, step, 0)

    for j in range(pieces):
        piece_copy(0, 0, j).wait()
    pl.semaphore_wait(barrier, 3 + env - 1)
    own_sends(0)
    for r in range(rounds):
        o_copy(r, 0).start()
    for r in range(rounds):
        o_copy(r, 1).start()
    trow = lax.broadcasted_iota(jnp.int32, tag.shape, 0)
    tag[...] = jnp.where(trow == 0, picks_ref[0, 0], picks_ref[0, 1]).astype(F32)
    for copy in pick_copies:
        copy.start()
    picks_all[ME] = tag[...]
    for b in range(1, blocks):
        for j in range(pieces):
            piece_copy(0, b, j).wait()

    row = lax.broadcasted_iota(jnp.int32, (count, count), 0)
    col = lax.broadcasted_iota(jnp.int32, (count, count), 1)
    order[...] = jnp.where(col == (row % envs) * steps + row // envs, 1.0, 0.0).astype(BF16)
    hid[...] = jnp.zeros_like(hid)
    ssq[...] = jnp.zeros_like(ssq)
    own_in.wait()
    norm(own_ref.at[0], rows.at[0, OWN])
    hop(0)
    for r in range(1, rounds):
        norm(own_ref.at[r], rows.at[r, OWN])
    hop(1)
    opp_in.wait()
    for r in range(rounds):
        norm(opp_ref.at[r], rows.at[r, ME])
    hop(2)
    lane_step = lax.broadcasted_iota(jnp.int32, (envs, steps, steps), 2)
    row_step = lax.broadcasted_iota(jnp.int32, (envs, steps, steps), 1)
    for r in range(rounds):
        hot = 0.0
        for side in range(2):
            ids = acts_ref[side, r].astype(F32)
            spread = jnp.where(lane_step == row_step, jnp.broadcast_to(ids[:, None, :], (envs, steps, steps)), 0.0)
            ids = jnp.sum(spread, axis=2, keepdims=True).reshape(count, 1)
            hot = hot + jnp.where(ids == lax.broadcasted_iota(jnp.int32, onehot.shape[1:], 1).astype(F32), 1.0, 0.0)
        onehot[r] = hot.astype(BF16)
    for r in range(rounds):
        o_copy(r, 1).wait_recv()
        norm(rows.at[r, SIB], rows.at[r, SIB])
    hop(3)
    for kind in (1, 2):
        for b in range(blocks):
            for j in range(pieces):
                piece_copy(kind, b, j).wait()
    for copy in pick_copies:
        copy.wait_recv()

    def s_copy(b, r, k):
        return remote(to_sib.at[b, k, r], from_sib.at[b, k, r], s_send.at[b, r, k], s_recv.at[b, r, k], sib, me)

    def x_copy(b, r):
        return remote(to_x.at[b, r], from_x.at[b, r], x_send.at[b, r], x_recv.at[b, r], across, me)

    mine = league_me.astype(F32)

    def column(b, j):
        return pl.ds(pl.multiple_of(dest(b, j) * share + (b % 2) * lane, lane), lane)

    def unit(b, r):
        @pl.when(b == 0)
        def _():
            o_copy(r, 0).wait_recv()
            o_copy(r, 2).start()
            o_copy(r, 2).wait_recv()
            norm(rows.at[r, DIAG], rows.at[r, DIAG])
            o_copy(r, 2).wait_send()
            norm(rows.at[r, ACROSS], rows.at[r, ACROSS])

        @pl.when(jnp.logical_and(b == 0, r == 0))
        def _():
            hop(4)

        @pl.when(r == 0)
        def _():
            for line in range(LINE):
                w_wait(b, line * PAIR + (1 - y))

        def dot(slot):
            return jnp.dot(
                rows[r, slot], wbuf[b].reshape(env * depth, width), preferred_element_type=F32
            )

        def served(slot):
            chosen = jnp.where(r == 0, picks_all[slot, 0:1, :], picks_all[slot, 1:2, :])[:, :1]
            return dot(slot) * jnp.where(chosen == mine, 1.0, 0.0)

        to_sib[b, 0, r] = served(DIAG).astype(BF16)
        s_copy(b, r, 0).start()
        to_x[b, r] = served(ACROSS).astype(BF16)
        to_sib[b, 1, r] = served(SIB).astype(BF16)
        s_copy(b, r, 1).start()
        s_copy(b, r, 0).wait_recv()
        to_x[b, r] = to_x[b, r] + from_sib[b, 0, r]
        x_copy(b, r).start()
        part[b, r] = jnp.dot(onehot[r], table[b], preferred_element_type=F32)
        part[b, r] += dot(OWN)
        part[b, r] += served(ME)
        for j in range(pieces):
            here = pl.ds(j * lane, lane)
            at = column(b, j)
            part[b, r, :, here] += own_ref[r, :, at].astype(F32) + opp_ref[r, :, at].astype(F32)

    def a_copy(b, r, j):
        target = dest(b, j)
        return remote(
            jsend.at[b, r, j], arecv.at[r, b % 2, me], a_send.at[b, r, j], a_recv.at[r, b % 2, me],
            league_me, target,
        )

    def a_each(b, r, do):
        for j in range(pieces):
            @pl.when(dest(b, j) != me)
            def _():
                do(j)

    tile = 64

    def finish(b, r):
        s_copy(b, r, 1).wait_recv()
        x_copy(b, r).wait_recv()
        gains = jnp.concatenate([vgain_ref[:, column(b, j)] for j in range(pieces)], axis=1).astype(F32)

        def joint_tile(i, _):
            at = pl.ds(pl.multiple_of(i * tile, tile), tile)
            v = part[b, r, at, :] + from_sib[b, 1, r, at, :].astype(F32) + from_x[b, r, at, :].astype(F32)
            ssq[r, at, :] += jnp.broadcast_to(jnp.sum(v * v, axis=-1, keepdims=True), (tile, lane))
            jrow[r, at, :] = (v * gains).astype(BF16)
            return 0

        lax.fori_loop(0, count // tile, joint_tile, 0)
        moved = jnp.dot(order[...], jrow[r], preferred_element_type=F32).astype(BF16)
        for j in range(pieces):
            jsend[b, r, j] = moved[:, j * lane:(j + 1) * lane].reshape(steps, envs, lane)
        a_each(b, r, lambda j: a_copy(b, r, j).start())
        for j in range(pieces):
            @pl.when(dest(b, j) == me)
            def _():
                arecv[r, b % 2, me] = jsend[b, r, j]
        hid[r] += jnp.dot(jrow[r], up[b], preferred_element_type=F32)

    def stage(s, _):
        def one(q, _):
            @pl.when(jnp.logical_and(s == 2, q >= 2))
            def _():
                hop(8 + q)

            finish(q // rounds, q % rounds)
            return 0

        lax.fori_loop(jnp.where(s < 3, 0, 2 * s - 2), jnp.where(s < 2, 0, 2 * s), one, 0)

        @pl.when(s < blocks)
        def _():
            def each(r, _):
                unit(s, r)

                @pl.when(jnp.logical_and(s == 0, r == 0))
                def _():
                    hop(5)
                    hop(6)

                @pl.when(jnp.logical_and(s < 2, s + r > 0))
                def _():
                    hop(6 + 2 * s + r)

                return 0

            lax.fori_loop(0, rounds, each, 0)

        return 0

    lax.fori_loop(0, blocks + 1, stage, 0)

    row_env = lax.broadcasted_iota(jnp.int32, (count, lane), 0) // steps
    at_lane = lax.broadcasted_iota(jnp.int32, (count, lane), 1)

    def c_copy(r, d):
        return remote(
            sc_send.at[r], sc_recv.at[r, me], c_send.at[r, d], c_recv.at[r, me], league_me, (me + d) % env
        )

    for r in range(rounds):
        scale = lax.rsqrt(ssq[r] * (1.0 / model) + 1e-05)
        ssq[r] = scale
        placed = jnp.where(at_lane == me * envs + row_env, scale, 0.0)
        sc_send[r] = jnp.sum(placed.reshape(envs, steps, lane), axis=0)
        for d in range(1, env):
            c_copy(r, d).start()
        sc_recv[r, me] = sc_send[r]

    row_step = lax.broadcasted_iota(jnp.int32, (count, lane), 0) % steps
    for r in range(rounds):
        hidden = hid[r] * ssq[r][:, :1]
        hidden = (hidden / (1.0 + jnp.exp(-hidden))).astype(BF16).astype(F32)
        value = jnp.sum(hidden * vout_ref[...].astype(F32), axis=-1, keepdims=True)
        spread = jnp.where(at_lane == row_step, value, 0.0)
        val_ref[r] = jnp.sum(spread.reshape(envs, steps, lane), axis=1)[:, :steps]

    frow = lax.broadcasted_iota(jnp.int32, (lane, lane), 0)
    fcol = lax.broadcasted_iota(jnp.int32, (lane, lane), 1)
    same = jnp.where(frow == fcol, 1.0, 0.0).astype(BF16)
    for half in range(2):
        for r in range(rounds):
            for d in range(1, env):
                other = (me + d) % env
                remote(
                    jsend.at[0, r, 0], arecv.at[r, half, other], a_send.at[0, r, 0], a_recv.at[r, half, other],
                    league_me, other,
                ).wait_recv()

            def turn(t, _):
                piece = arecv[r, half, :, t].reshape(env * envs, lane)
                out_ref[r, t, half * lane:(half + 1) * lane, :] = lax.dot_general(
                    same, piece, (((1,), (1,)), ((), ())), preferred_element_type=F32
                ).astype(BF16)
                return 0

            lax.fori_loop(0, steps, turn, 0)
    for r in range(rounds):
        total = sc_recv[r, me]
        for d in range(1, env):
            other = (me + d) % env
            remote(
                sc_send.at[r], sc_recv.at[r, other], c_send.at[r, d], c_recv.at[r, other], league_me, other
            ).wait_recv()
            total = total + sc_recv[r, other]
        scale_ref[r] = total

    for b in range(blocks):
        finish_w_sends(b)
        for r in range(rounds):
            s_copy(b, r, 0).wait_send()
            s_copy(b, r, 1).wait_send()
            x_copy(b, r).wait_send()
            a_each(b, r, lambda j: a_copy(b, r, j).wait_send())
    for copy in pick_copies:
        copy.wait_send()
    for r in range(rounds):
        o_copy(r, 0).wait_send()
        o_copy(r, 1).wait_send()
        for d in range(1, env):
            c_copy(r, d).wait_send()


def fused(
    obs_own,
    obs_opp,
    actions,
    opponent_picks,
    policy_weight,
    policy_gain,
    action_table,
    value_gain,
    value_up,
    value_out,
):
    rounds, envs, steps, model = obs_own.shape[1:]
    count = envs * steps
    env = lax.axis_size("env")
    depth = policy_weight.shape[1]
    width = model // BLOCKS
    share = model // env
    lane = share // 2
    pieces = width // lane
    hidden = value_up.shape[1]
    choices = action_table.shape[0]
    vmem = pl.BlockSpec(memory_space=pltpu.VMEM)
    smem = pl.BlockSpec(memory_space=pltpu.SMEM)
    hbm = pl.BlockSpec(memory_space=pl.ANY)
    dma = pltpu.SemaphoreType.DMA
    turned, scales, val = pl.pallas_call(
        window_kernel,
        out_shape=(
            jax.ShapeDtypeStruct((rounds, steps, share, env * envs), BF16),
            jax.ShapeDtypeStruct((rounds, steps, lane), F32),
            jax.ShapeDtypeStruct((rounds, envs, steps), F32),
        ),
        in_specs=[hbm, hbm, hbm, vmem, smem, vmem, vmem, vmem, hbm, hbm],
        out_specs=(vmem, vmem, vmem),
        scratch_shapes=[
            pltpu.VMEM((BLOCKS, env, depth, width), BF16),
            pltpu.VMEM((rounds, 5, count, model), BF16),
            pltpu.VMEM((rounds, count, model), BF16),
            pltpu.VMEM((rounds, count, model), BF16),
            pltpu.VMEM((BLOCKS, choices, width), BF16),
            pltpu.VMEM((BLOCKS, width, hidden), BF16),
            pltpu.VMEM((8, 128), F32),
            pltpu.VMEM((5, 8, 128), F32),
            pltpu.VMEM((rounds, count, choices), BF16),
            pltpu.VMEM((count, count), BF16),
            pltpu.VMEM((BLOCKS, 2, rounds, count, width), BF16),
            pltpu.VMEM((BLOCKS, 2, rounds, count, width), BF16),
            pltpu.VMEM((BLOCKS, rounds, count, width), BF16),
            pltpu.VMEM((BLOCKS, rounds, count, width), BF16),
            pltpu.VMEM((BLOCKS, rounds, count, width), F32),
            pltpu.VMEM((rounds, count, lane), F32),
            pltpu.VMEM((rounds, count, hidden), F32),
            pltpu.VMEM((rounds, count, width), BF16),
            pltpu.VMEM((BLOCKS, rounds, pieces, steps, envs, lane), BF16),
            pltpu.VMEM((rounds, 2, env, steps, envs, lane), BF16),
            pltpu.VMEM((rounds, steps, lane), F32),
            pltpu.VMEM((rounds, env, steps, lane), F32),
            dma((2,)),
            dma((3, BLOCKS, pieces)),
            dma((BLOCKS, LINE, 3)),
            dma((BLOCKS, env)),
            dma((3, rounds)),
            dma((3, rounds)),
            dma((5,)),
            dma((5,)),
            dma((BLOCKS, rounds, 2)),
            dma((BLOCKS, rounds, 2)),
            dma((BLOCKS, rounds)),
            dma((BLOCKS, rounds)),
            dma((BLOCKS, rounds, pieces)),
            dma((rounds, 2, env)),
            dma((rounds, env)),
            dma((rounds, env)),
        ],
        compiler_params=pltpu.CompilerParams(
            collective_id=0, has_side_effects=True, vmem_limit_bytes=62 * MIB
        ),
    )(
        policy_weight[0],
        obs_own[0].reshape(rounds, count, model),
        obs_opp[0].reshape(rounds, count, model),
        actions[0],
        opponent_picks,
        policy_gain,
        value_gain[None],
        value_out[None],
        action_table,
        value_up,
    )
    out = (turned.astype(F32) * scales[:, :, None, :]).astype(BF16)
    return (out[None], val[None])


def solution(mesh):
    in_specs = (
        P("league", None, "env", None, None),
        P("league", None, "env", None, None),
        P("league", None, None, "env", None),
        P("league", None),
        P("league", "env", None),
        P("league", None),
        P(),
        P(),
        P(),
        P(),
    )
    out_specs = (P("league", None, None, "env", None), P("league", None, "env", None))
    body = fused if mesh.shape["env"] == LINE * PAIR else local
    return jax.shard_map(body, mesh=mesh, in_specs=in_specs, out_specs=out_specs, check_vma=False)
```

```python
import functools

import jax
import jax.numpy as jnp
from jax import lax
from jax.experimental import pallas as pl
from jax.experimental.pallas import tpu as pltpu
from jax.sharding import PartitionSpec as P

F32 = jnp.float32
BF16 = jnp.bfloat16
BLOCKS = 8
LINE = 4
PAIR = 2
MIB = 1 << 20
OWN, ME, SIB, ACROSS, DIAG = range(5)
MESH = pl.DeviceIdType.MESH


def rms_norm(inputs, gain):
    scale = lax.rsqrt(jnp.mean(inputs * inputs, axis=-1, keepdims=True) + 1e-05)
    return inputs * scale * gain.astype(jnp.float32)


def local(
    obs_own,
    obs_opp,
    actions,
    opponent_picks,
    policy_weight,
    policy_gain,
    action_table,
    value_gain,
    value_up,
    value_out,
):
    round_count = obs_own.shape[1]
    env_count = obs_own.shape[2]
    step_count = obs_own.shape[3]
    model_width = obs_own.shape[4]
    row_count = env_count * step_count
    weight_shard = policy_weight[0]
    own_gain = policy_gain[0]
    group_count = lax.axis_size("league")
    my_group = lax.axis_index("league")
    own_inputs = obs_own[0].reshape(round_count * row_count, model_width).astype(jnp.float32)
    own_normed = rms_norm(own_inputs, own_gain).astype(jnp.bfloat16)
    own_whole = lax.all_gather(weight_shard, "env", axis=0, tiled=True)
    own_state = own_inputs + jnp.dot(own_normed, own_whole, preferred_element_type=jnp.float32)
    every_pick = lax.all_gather(opponent_picks, "league", axis=0, tiled=True)
    action_range = jnp.arange(action_table.shape[0], dtype=jnp.int32)
    traj_list = []
    value_list = []
    for round_index in range(round_count):
        opp_raw = obs_opp[0, round_index].reshape(row_count, model_width)
        opp_inputs = opp_raw.astype(jnp.float32)
        all_rows = lax.all_gather(opp_raw, "league", axis=0, tiled=True)
        all_normed = rms_norm(all_rows.astype(jnp.float32), own_gain).astype(jnp.bfloat16)
        products = jnp.dot(all_normed, own_whole, preferred_element_type=jnp.float32)
        served = (every_pick[:, round_index] == my_group).astype(jnp.float32)
        products = (
            products.reshape(group_count, row_count, model_width) * served[:, None, None]
        ).astype(jnp.bfloat16)
        answers = lax.all_to_all(products, "league", split_axis=0, concat_axis=0, tiled=True)
        opp_state = opp_inputs + jnp.sum(answers.astype(jnp.float32), axis=0)
        own_ids = actions[0, 0, round_index].reshape(row_count)
        opp_ids = actions[0, 1, round_index].reshape(row_count)
        onehot = (own_ids[:, None] == action_range[None, :]).astype(jnp.bfloat16) + (
            opp_ids[:, None] == action_range[None, :]
        ).astype(jnp.bfloat16)
        action_sum = jnp.dot(onehot, action_table, preferred_element_type=jnp.float32)
        round_state = lax.dynamic_slice_in_dim(own_state, round_index * row_count, row_count, 0)
        joint_sum = round_state + opp_state + action_sum
        joint_row = rms_norm(joint_sum, value_gain).astype(jnp.bfloat16)
        value_hidden = jax.nn.silu(
            jnp.dot(joint_row, value_up, preferred_element_type=jnp.float32)
        ).astype(jnp.bfloat16)
        value_est = jnp.dot(value_hidden, value_out, preferred_element_type=jnp.float32)
        value_list.append(value_est.reshape(env_count, step_count))
        time_block = joint_row.reshape(env_count, step_count, model_width).transpose(1, 2, 0)
        traj_list.append(lax.all_to_all(time_block, "env", split_axis=1, concat_axis=2, tiled=True))
    learner_rows = jnp.stack(traj_list)
    values = jnp.stack(value_list)
    return (learner_rows[None], values[None])


PLAN = (
    3309632, 5247137, 169935878, 33561763, 102858760, 136324224, 172068930, 173150218,
    70266891, 174077030, 14851206, 101727265, 105922659, 135371844, 17962115, 110207111,
    142624992, 20154505, 72372452, 241282154, 145893397, 238049505, 268459237, 274993410,
    273943809, 114405446, 147992775, 209888424, 115416265, 149071983, 211987599, 181579979,
    182662348, 217266351,
)
TURN = 8
FIRST = 2
BALANCE = 2
AHEAD = 2


def pair(b):
    return (b // 2 + FIRST) % LINE


def dest(b, j):
    return pair(b) if j == 0 else LINE * PAIR - 1 - pair(b)


def interior(b):
    return pair(b) >= PAIR


def window_kernel(
    w_hbm, own_hbm, opp_hbm, acts_ref, picks_ref, gain_ref, vgain_ref, vout_ref, table_hbm, up_hbm,
    out_ref, scale_ref, val_ref,
    wbuf, rows, own_ref, opp_ref, table, up, tag, picks_all, onehot, order,
    to_sib, from_sib, to_x, from_x, part, ssq, hid, jrow, jsend, arecv, sc_send, sc_recv,
    l_sem, b_sem, w_send, w_recv, e_send, o_send, o_recv, p_send, p_recv, s_send, s_recv, x_send, x_recv,
    a_send, a_recv, c_send, c_recv,
):
    blocks, env, depth, width = wbuf.shape
    rounds, count, model = own_ref.shape
    pieces, steps, envs, lane = jsend.shape[2:]
    share = model // env
    league_me = lax.axis_index("league")
    me = lax.axis_index("env")
    x, core = league_me // 2, league_me % 2
    z, y = me // PAIR, me % PAIR
    sib = x * 2 + (1 - core)
    across = (1 - x) * 2 + core
    diag = (1 - x) * 2 + (1 - core)
    y_peer = z * PAIR + (1 - y)

    barrier = pltpu.get_barrier_semaphore()
    for group in (sib, across, diag):
        pl.semaphore_signal(barrier, inc=1, device_id=(group, me), device_id_type=MESH)
    for d in range(1, env):
        pl.semaphore_signal(barrier, inc=1, device_id=(league_me, (me + d) % env), device_id_type=MESH)

    def piece_copy(kind, b, j):
        start = pl.multiple_of(dest(b, j) * share + (b % 2) * lane, lane)
        cols = pl.ds(j * lane, lane)
        if kind == 0:
            src, dst = w_hbm.at[:, pl.ds(start, lane)], wbuf.at[b, me, :, cols]
        elif kind == 1:
            src, dst = table_hbm.at[:, pl.ds(start, lane)], table.at[b, :, cols]
        else:
            src, dst = up_hbm.at[pl.ds(start, lane)], up.at[b, cols]
        return pltpu.make_async_copy(src, dst, b_sem.at[kind, b, j])

    own_in = pltpu.make_async_copy(own_hbm, own_ref, l_sem.at[0])
    opp_in = pltpu.make_async_copy(opp_hbm, opp_ref, l_sem.at[1])
    for b in range(blocks):
        for j in range(pieces):
            piece_copy(0, b, j).start()
    own_in.start()
    opp_in.start()
    for kind in (1, 2):
        for b in range(blocks):
            for j in range(pieces):
                piece_copy(kind, b, j).start()

    def remote(src, dst, send, recv, group, place):
        return pltpu.make_async_remote_copy(
            src_ref=src, dst_ref=dst, send_sem=send, recv_sem=recv,
            device_id=(group, place), device_id_type=MESH,
        )

    def w_copy(b, line, way, place):
        slot = line * PAIR + y
        return remote(
            wbuf.at[b, slot], wbuf.at[b, slot], w_send.at[b, line, way], w_recv.at[b, slot], league_me, place
        )

    def to_right(b, line):
        return w_copy(b, line, 0, me + PAIR)

    def to_left(b, line):
        return w_copy(b, line, 1, me - PAIR)

    def to_y(b, line):
        return w_copy(b, line, 2, y_peer)

    def w_wait(b, slot):
        remote(
            wbuf.at[b, slot], wbuf.at[b, slot], w_send.at[b, 0, 2], w_recv.at[b, slot], league_me, y_peer
        ).wait_recv()

    def own_sends(b):
        @pl.when(z < LINE - 1)
        def _():
            to_right(b, z).start()

        @pl.when(z > 0)
        def _():
            to_left(b, z).start()

        to_y(b, z).start()

    def by_z(b, line):
        return jnp.logical_or(
            jnp.logical_and(line == z - 1, jnp.logical_or(z == 1, jnp.logical_and(z == LINE - 1, b % BALANCE == 1))),
            jnp.logical_and(line == z + 1, jnp.logical_or(z == LINE - 2, jnp.logical_and(z == 0, b % BALANCE == 1))),
        )

    def other(b, place):
        slot = z * PAIR + 1 - y
        return remote(wbuf.at[b, slot], wbuf.at[b, slot], e_send.at[b], w_recv.at[b, slot], league_me, place)

    def goes_right(b):
        return jnp.logical_or(z == 0, jnp.logical_and(z == LINE - 2, b % BALANCE == 1))

    def goes_left(b):
        return jnp.logical_or(z == LINE - 1, jnp.logical_and(z == 1, b % BALANCE == 1))

    def hop(k):
        b, h = k // (LINE - 1), k % (LINE - 1) + 1
        low, high = z - h, z + h

        @pl.when(low >= 0)
        def _():
            w_wait(b, low * PAIR + y)

            @pl.when(z < LINE - 1)
            def _():
                to_right(b, low).start()

            @pl.when(jnp.logical_not(by_z(b, low)))
            def _():
                to_y(b, low).start()

        @pl.when(high < LINE)
        def _():
            w_wait(b, high * PAIR + y)

            @pl.when(z > 0)
            def _():
                to_left(b, high).start()

            @pl.when(jnp.logical_not(by_z(b, high)))
            def _():
                to_y(b, high).start()

        @pl.when(h == 1)
        def _():
            w_wait(b, z * PAIR + 1 - y)

            @pl.when(goes_right(b))
            def _():
                other(b, me + PAIR).start()

            @pl.when(goes_left(b))
            def _():
                other(b, me - PAIR).start()

        @pl.when(jnp.logical_and(h == 2, b < blocks - AHEAD))
        def _():
            own_sends(b + AHEAD)

    def finish_w_sends(b):
        for line in range(LINE):
            @pl.when(jnp.logical_and(line <= z, z < LINE - 1))
            def _():
                to_right(b, line).wait_send()

            @pl.when(jnp.logical_and(line >= z, z > 0))
            def _():
                to_left(b, line).wait_send()

            @pl.when(jnp.logical_not(by_z(b, line)))
            def _():
                to_y(b, line).wait_send()

        @pl.when(jnp.logical_or(goes_right(b), goes_left(b)))
        def _():
            other(b, y_peer).wait_send()

    def o_copy(r, way):
        if way == 0:
            src, dst, group = opp_hbm.at[r], rows.at[r, ACROSS], across
        elif way == 1:
            src, dst, group = opp_hbm.at[r], rows.at[r, SIB], sib
        else:
            src, dst, group = rows.at[r, ACROSS], rows.at[r, DIAG], sib
        return remote(src, dst, o_send.at[way, r], o_recv.at[way, r], group, me)

    pick_copies = [
        remote(tag, picks_all.at[slot], p_send.at[slot], p_recv.at[slot], group, me)
        for slot, group in ((SIB, sib), (ACROSS, across), (DIAG, diag))
    ]

    def norm(src, dst, tile=64):
        def step(i, _):
            at = pl.ds(pl.multiple_of(i * tile, tile), tile)
            v = src[at, :].astype(F32)
            scale = lax.rsqrt(jnp.mean(v * v, axis=-1, keepdims=True) + 1e-05)
            dst[at, :] = (v * scale * gain_ref[...].astype(F32)).astype(BF16)
            return 0

        lax.fori_loop(0, count // tile, step, 0)

    for b in range(AHEAD):
        for j in range(pieces):
            piece_copy(0, b, j).wait()
    trow = lax.broadcasted_iota(jnp.int32, tag.shape, 0)
    tag[...] = jnp.where(trow == 0, picks_ref[0, 0], picks_ref[0, 1]).astype(F32)
    picks_all[ME] = tag[...]
    pl.semaphore_wait(barrier, 3 + env - 1)
    for copy in pick_copies:
        copy.start()
    for b in range(AHEAD):
        own_sends(b)
    for r in range(rounds):
        o_copy(r, 0).start()
    for r in range(rounds):
        o_copy(r, 1).start()
    for b in range(AHEAD, blocks):
        for j in range(pieces):
            piece_copy(0, b, j).wait()

    row = lax.broadcasted_iota(jnp.int32, (count, count), 0)
    col = lax.broadcasted_iota(jnp.int32, (count, count), 1)
    order[...] = jnp.where(col == (row % envs) * steps + row // envs, 1.0, 0.0).astype(BF16)
    hid[...] = jnp.zeros_like(hid)
    ssq[...] = jnp.zeros_like(ssq)
    own_in.wait()
    norm(own_ref.at[0], rows.at[0, OWN])
    hop(0)
    for r in range(1, rounds):
        norm(own_ref.at[r], rows.at[r, OWN])
    hop(1)
    opp_in.wait()
    for r in range(rounds):
        norm(opp_ref.at[r], rows.at[r, ME])
    hop(2)
    lane_step = lax.broadcasted_iota(jnp.int32, (envs, steps, steps), 2)
    row_step = lax.broadcasted_iota(jnp.int32, (envs, steps, steps), 1)
    for r in range(rounds):
        hot = 0.0
        for side in range(2):
            ids = acts_ref[side, r].astype(F32)
            spread = jnp.where(lane_step == row_step, jnp.broadcast_to(ids[:, None, :], (envs, steps, steps)), 0.0)
            ids = jnp.sum(spread, axis=2, keepdims=True).reshape(count, 1)
            hot = hot + jnp.where(ids == lax.broadcasted_iota(jnp.int32, onehot.shape[1:], 1).astype(F32), 1.0, 0.0)
        onehot[r] = hot.astype(BF16)
    for r in range(rounds):
        o_copy(r, 1).wait_recv()
        norm(rows.at[r, SIB], rows.at[r, SIB])
    for kind in (1, 2):
        for b in range(blocks):
            for j in range(pieces):
                piece_copy(kind, b, j).wait()
    for copy in pick_copies:
        copy.wait_recv()

    def s_copy(b, r, k):
        return remote(to_sib.at[b, k, r], from_sib.at[b, k, r], s_send.at[b, r, k], s_recv.at[b, r, k], sib, me)

    def x_copy(b, r):
        return remote(to_x.at[b, r], from_x.at[b, r], x_send.at[b, r], x_recv.at[b, r], across, me)

    mine = league_me.astype(F32)

    def column(b, j):
        return pl.ds(pl.multiple_of(dest(b, j) * share + (b % 2) * lane, lane), lane)

    def arrive(r):
        o_copy(r, 0).wait_recv()
        o_copy(r, 2).start()
        o_copy(r, 2).wait_recv()
        norm(rows.at[r, DIAG], rows.at[r, DIAG])
        o_copy(r, 2).wait_send()
        norm(rows.at[r, ACROSS], rows.at[r, ACROSS])

    def ready(b):
        for line in range(LINE):
            @pl.when(line != z)
            def _():
                w_wait(b, line * PAIR + (1 - y))

    def dot(b, r, slot):
        return jnp.dot(rows[r, slot], wbuf[b].reshape(env * depth, width), preferred_element_type=F32)

    def served(b, r, slot):
        chosen = jnp.where(r == 0, picks_all[slot, 0:1, :], picks_all[slot, 1:2, :])[:, :1]
        return dot(b, r, slot) * jnp.where(chosen == mine, 1.0, 0.0)

    def for_diag(b, r):
        to_sib[b, 0, r] = served(b, r, DIAG).astype(BF16)
        s_copy(b, r, 0).start()

    def for_across(b, r):
        to_x[b, r] = served(b, r, ACROSS).astype(BF16)
        s_copy(b, r, 0).wait_recv()
        to_x[b, r] = to_x[b, r] + from_sib[b, 0, r]
        x_copy(b, r).start()

    def here(b, r):
        to_sib[b, 1, r] = served(b, r, SIB).astype(BF16)
        s_copy(b, r, 1).start()
        part[b, r] = jnp.dot(onehot[r], table[b], preferred_element_type=F32)
        part[b, r] += dot(b, r, OWN)
        part[b, r] += served(b, r, ME)
        for j in range(pieces):
            cols = pl.ds(j * lane, lane)
            at = column(b, j)
            part[b, r, :, cols] += own_ref[r, :, at].astype(F32) + opp_ref[r, :, at].astype(F32)

    def a_copy(b, r, j):
        target = dest(b, j)
        return remote(
            jsend.at[b, r, j], arecv.at[r, b % 2, me], a_send.at[b, r, j], a_recv.at[r, b % 2, me],
            league_me, target,
        )

    def a_each(b, r, do, near=True, far=True):
        for j in range(pieces):
            crosses = dest(b, j) % PAIR != y

            @pl.when(jnp.logical_and(dest(b, j) != me, jnp.where(crosses, far, near)))
            def _():
                do(j)

    tile = 64

    def finish(b, r, now):
        s_copy(b, r, 1).wait_recv()
        x_copy(b, r).wait_recv()
        gains = jnp.concatenate([vgain_ref[:, column(b, j)] for j in range(pieces)], axis=1).astype(F32)

        def joint_tile(i, _):
            at = pl.ds(pl.multiple_of(i * tile, tile), tile)
            v = part[b, r, at, :] + from_sib[b, 1, r, at, :].astype(F32) + from_x[b, r, at, :].astype(F32)
            ssq[r, at, :] += jnp.broadcast_to(jnp.sum(v * v, axis=-1, keepdims=True), (tile, lane))
            jrow[r, at, :] = (v * gains).astype(BF16)
            return 0

        lax.fori_loop(0, count // tile, joint_tile, 0)
        moved = jnp.dot(order[...], jrow[r], preferred_element_type=F32).astype(BF16)
        for j in range(pieces):
            jsend[b, r, j] = moved[:, j * lane:(j + 1) * lane].reshape(steps, envs, lane)
        a_each(b, r, lambda j: a_copy(b, r, j).start(), near=jnp.logical_or(now, interior(b)), far=now)
        for j in range(pieces):
            @pl.when(dest(b, j) == me)
            def _():
                arecv[r, b % 2, me] = jsend[b, r, j]
        hid[r] += jnp.dot(jrow[r], up[b], preferred_element_type=F32)

    def release(b, r):
        a_each(b, r, lambda j: a_copy(b, r, j).start(), near=jnp.logical_not(interior(b)))

    def choose_at(i, values, start, stop):
        if stop - start == 1:
            return jnp.int32(values[start])
        middle = (start + stop) // 2
        return jnp.where(i < middle, choose_at(i, values, start, middle), choose_at(i, values, middle, stop))

    def act(i, _):
        word = choose_at(lax.div(i, 3), PLAN, 0, len(PLAN))
        turn = lax.rem(i, 3)
        code = lax.rem(jnp.where(turn == 0, word, jnp.where(turn == 1, lax.div(word, 1024), lax.div(word, 1024 * 1024))), 1024)
        kind, arg = lax.div(code, 32), lax.rem(code, 32)
        b, r = lax.div(arg, rounds), lax.rem(arg, rounds)
        for k, do in enumerate((
            lambda: hop(arg), lambda: arrive(arg), lambda: ready(arg), lambda: for_diag(b, r),
            lambda: for_across(b, r), lambda: here(b, r), lambda: finish(b, r, kind == 6), None,
            lambda: release(b, r),
        )):
            if do is not None:
                pl.when(jnp.logical_or(kind == 6, kind == 7) if k == 6 else kind == k)(do)

        return 0

    lax.fori_loop(0, 3 * len(PLAN), act, 0)

    def w_sent(b, _):
        finish_w_sends(b)
        return 0

    lax.fori_loop(0, blocks, w_sent, 0)
    row_env = lax.broadcasted_iota(jnp.int32, (count, lane), 0) // steps
    at_lane = lax.broadcasted_iota(jnp.int32, (count, lane), 1)

    def c_copy(r, d):
        return remote(
            sc_send.at[r], sc_recv.at[r, me], c_send.at[r, d], c_recv.at[r, me], league_me, (me + d) % env
        )

    for r in range(rounds):
        scale = lax.rsqrt(ssq[r] * (1.0 / model) + 1e-05)
        ssq[r] = scale
        placed = jnp.where(at_lane == me * envs + row_env, scale, 0.0)
        sc_send[r] = jnp.sum(placed.reshape(envs, steps, lane), axis=0)
        for d in range(1, env):
            c_copy(r, d).start()
        sc_recv[r, me] = sc_send[r]

    row_step = lax.broadcasted_iota(jnp.int32, (count, lane), 0) % steps
    for r in range(rounds):
        hidden = hid[r] * ssq[r][:, :1]
        hidden = (hidden / (1.0 + jnp.exp(-hidden))).astype(BF16).astype(F32)
        value = jnp.sum(hidden * vout_ref[...].astype(F32), axis=-1, keepdims=True)
        spread = jnp.where(at_lane == row_step, value, 0.0)
        val_ref[r] = jnp.sum(spread.reshape(envs, steps, lane), axis=1)[:, :steps]

    for half in range(2):
        for r in range(rounds):
            for d in range(1, env):
                peer = (me + d) % env
                remote(
                    jsend.at[0, r, 0], arecv.at[r, half, peer], a_send.at[0, r, 0], a_recv.at[r, half, peer],
                    league_me, peer,
                ).wait_recv()

            def turn(i, _):
                for t in range(TURN):
                    piece = arecv[r, half, :, i * TURN + t].reshape(env * envs, lane)
                    out_ref[r, i * TURN + t, half * lane:(half + 1) * lane, :] = piece.T
                return 0

            lax.fori_loop(0, steps // TURN, turn, 0)
    for r in range(rounds):
        total = sc_recv[r, me]
        for d in range(1, env):
            peer = (me + d) % env
            remote(
                sc_send.at[r], sc_recv.at[r, peer], c_send.at[r, d], c_recv.at[r, peer], league_me, peer
            ).wait_recv()
            total = total + sc_recv[r, peer]
        scale_ref[r] = total

    def sent(q, _):
        b, r = q // rounds, q % rounds
        s_copy(b, r, 0).wait_send()
        s_copy(b, r, 1).wait_send()
        x_copy(b, r).wait_send()
        a_each(b, r, lambda j: a_copy(b, r, j).wait_send())
        return 0

    lax.fori_loop(0, blocks * rounds, sent, 0)
    for copy in pick_copies:
        copy.wait_send()
    for r in range(rounds):
        o_copy(r, 0).wait_send()
        o_copy(r, 1).wait_send()
        for d in range(1, env):
            c_copy(r, d).wait_send()


def fused(
    obs_own,
    obs_opp,
    actions,
    opponent_picks,
    policy_weight,
    policy_gain,
    action_table,
    value_gain,
    value_up,
    value_out,
):
    rounds, envs, steps, model = obs_own.shape[1:]
    count = envs * steps
    env = lax.axis_size("env")
    depth = policy_weight.shape[1]
    width = model // BLOCKS
    share = model // env
    lane = share // 2
    pieces = width // lane
    hidden = value_up.shape[1]
    choices = action_table.shape[0]
    vmem = pl.BlockSpec(memory_space=pltpu.VMEM)
    smem = pl.BlockSpec(memory_space=pltpu.SMEM)
    hbm = pl.BlockSpec(memory_space=pl.ANY)
    dma = pltpu.SemaphoreType.DMA
    turned, scales, val = pl.pallas_call(
        window_kernel,
        out_shape=(
            jax.ShapeDtypeStruct((rounds, steps, share, env * envs), BF16),
            jax.ShapeDtypeStruct((rounds, steps, lane), F32),
            jax.ShapeDtypeStruct((rounds, envs, steps), F32),
        ),
        in_specs=[hbm, hbm, hbm, vmem, smem, vmem, vmem, vmem, hbm, hbm],
        out_specs=(vmem, vmem, vmem),
        scratch_shapes=[
            pltpu.VMEM((BLOCKS, env, depth, width), BF16),
            pltpu.VMEM((rounds, 5, count, model), BF16),
            pltpu.VMEM((rounds, count, model), BF16),
            pltpu.VMEM((rounds, count, model), BF16),
            pltpu.VMEM((BLOCKS, choices, width), BF16),
            pltpu.VMEM((BLOCKS, width, hidden), BF16),
            pltpu.VMEM((8, 128), F32),
            pltpu.VMEM((5, 8, 128), F32),
            pltpu.VMEM((rounds, count, choices), BF16),
            pltpu.VMEM((count, count), BF16),
            pltpu.VMEM((BLOCKS, 2, rounds, count, width), BF16),
            pltpu.VMEM((BLOCKS, 2, rounds, count, width), BF16),
            pltpu.VMEM((BLOCKS, rounds, count, width), BF16),
            pltpu.VMEM((BLOCKS, rounds, count, width), BF16),
            pltpu.VMEM((BLOCKS, rounds, count, width), F32),
            pltpu.VMEM((rounds, count, lane), F32),
            pltpu.VMEM((rounds, count, hidden), F32),
            pltpu.VMEM((rounds, count, width), BF16),
            pltpu.VMEM((BLOCKS, rounds, pieces, steps, envs, lane), BF16),
            pltpu.VMEM((rounds, 2, env, steps, envs, lane), BF16),
            pltpu.VMEM((rounds, steps, lane), F32),
            pltpu.VMEM((rounds, env, steps, lane), F32),
            dma((2,)),
            dma((3, BLOCKS, pieces)),
            dma((BLOCKS, LINE, 3)),
            dma((BLOCKS, env)),
            dma((BLOCKS,)),
            dma((3, rounds)),
            dma((3, rounds)),
            dma((5,)),
            dma((5,)),
            dma((BLOCKS, rounds, 2)),
            dma((BLOCKS, rounds, 2)),
            dma((BLOCKS, rounds)),
            dma((BLOCKS, rounds)),
            dma((BLOCKS, rounds, pieces)),
            dma((rounds, 2, env)),
            dma((rounds, env)),
            dma((rounds, env)),
        ],
        compiler_params=pltpu.CompilerParams(
            collective_id=0, has_side_effects=True, vmem_limit_bytes=62 * MIB
        ),
    )(
        policy_weight[0],
        obs_own[0].reshape(rounds, count, model),
        obs_opp[0].reshape(rounds, count, model),
        actions[0],
        opponent_picks,
        policy_gain,
        value_gain[None],
        value_out[None],
        action_table,
        value_up,
    )
    out = (turned.astype(F32) * scales[:, :, None, :]).astype(BF16)
    return (out[None], val[None])


def solution(mesh):
    in_specs = (
        P("league", None, "env", None, None),
        P("league", None, "env", None, None),
        P("league", None, None, "env", None),
        P("league", None),
        P("league", "env", None),
        P("league", None),
        P(),
        P(),
        P(),
        P(),
    )
    out_specs = (P("league", None, None, "env", None), P("league", None, "env", None))
    body = fused if mesh.shape["env"] == LINE * PAIR else local
    return jax.shard_map(body, mesh=mesh, in_specs=in_specs, out_specs=out_specs, check_vma=False)
```

```python
import functools

import jax
import jax.numpy as jnp
from jax import lax
from jax.experimental import pallas as pl
from jax.experimental.pallas import tpu as pltpu
from jax.sharding import PartitionSpec as P

F32 = jnp.float32
BF16 = jnp.bfloat16
BLOCKS = 8
LINE = 4
PAIR = 2
MIB = 1 << 20
OWN, ME, SIB, ACROSS, DIAG = range(5)
MESH = pl.DeviceIdType.MESH


def rms_norm(inputs, gain):
    scale = lax.rsqrt(jnp.mean(inputs * inputs, axis=-1, keepdims=True) + 1e-05)
    return inputs * scale * gain.astype(jnp.float32)


def local(
    obs_own,
    obs_opp,
    actions,
    opponent_picks,
    policy_weight,
    policy_gain,
    action_table,
    value_gain,
    value_up,
    value_out,
):
    round_count = obs_own.shape[1]
    env_count = obs_own.shape[2]
    step_count = obs_own.shape[3]
    model_width = obs_own.shape[4]
    row_count = env_count * step_count
    weight_shard = policy_weight[0]
    own_gain = policy_gain[0]
    group_count = lax.axis_size("league")
    my_group = lax.axis_index("league")
    own_inputs = obs_own[0].reshape(round_count * row_count, model_width).astype(jnp.float32)
    own_normed = rms_norm(own_inputs, own_gain).astype(jnp.bfloat16)
    own_whole = lax.all_gather(weight_shard, "env", axis=0, tiled=True)
    own_state = own_inputs + jnp.dot(own_normed, own_whole, preferred_element_type=jnp.float32)
    every_pick = lax.all_gather(opponent_picks, "league", axis=0, tiled=True)
    action_range = jnp.arange(action_table.shape[0], dtype=jnp.int32)
    traj_list = []
    value_list = []
    for round_index in range(round_count):
        opp_raw = obs_opp[0, round_index].reshape(row_count, model_width)
        opp_inputs = opp_raw.astype(jnp.float32)
        all_rows = lax.all_gather(opp_raw, "league", axis=0, tiled=True)
        all_normed = rms_norm(all_rows.astype(jnp.float32), own_gain).astype(jnp.bfloat16)
        products = jnp.dot(all_normed, own_whole, preferred_element_type=jnp.float32)
        served = (every_pick[:, round_index] == my_group).astype(jnp.float32)
        products = (
            products.reshape(group_count, row_count, model_width) * served[:, None, None]
        ).astype(jnp.bfloat16)
        answers = lax.all_to_all(products, "league", split_axis=0, concat_axis=0, tiled=True)
        opp_state = opp_inputs + jnp.sum(answers.astype(jnp.float32), axis=0)
        own_ids = actions[0, 0, round_index].reshape(row_count)
        opp_ids = actions[0, 1, round_index].reshape(row_count)
        onehot = (own_ids[:, None] == action_range[None, :]).astype(jnp.bfloat16) + (
            opp_ids[:, None] == action_range[None, :]
        ).astype(jnp.bfloat16)
        action_sum = jnp.dot(onehot, action_table, preferred_element_type=jnp.float32)
        round_state = lax.dynamic_slice_in_dim(own_state, round_index * row_count, row_count, 0)
        joint_sum = round_state + opp_state + action_sum
        joint_row = rms_norm(joint_sum, value_gain).astype(jnp.bfloat16)
        value_hidden = jax.nn.silu(
            jnp.dot(joint_row, value_up, preferred_element_type=jnp.float32)
        ).astype(jnp.bfloat16)
        value_est = jnp.dot(value_hidden, value_out, preferred_element_type=jnp.float32)
        value_list.append(value_est.reshape(env_count, step_count))
        time_block = joint_row.reshape(env_count, step_count, model_width).transpose(1, 2, 0)
        traj_list.append(lax.all_to_all(time_block, "env", split_axis=1, concat_axis=2, tiled=True))
    learner_rows = jnp.stack(traj_list)
    values = jnp.stack(value_list)
    return (learner_rows[None], values[None])


PLAN = (
    167837699, 5247137, 169935878, 8555527, 102858784, 136445961, 104925194, 173026468,
    13643908, 107023374, 175127718, 17842310, 103908385, 108106770, 135372868, 20030595,
    142744709, 21112032, 239247586, 241345557, 111219734, 24291435, 272894208, 145893638,
    204647617, 113318085, 208842861, 181548172, 74654920, 211926126, 150091950, 214117551,
    217266381,
)
TURN = 8
FIRST = 2
BALANCE = 2
AHEAD = 2


def pair(b):
    return (b // 2 + FIRST) % LINE


def dest(b, j):
    return pair(b) if j == 0 else LINE * PAIR - 1 - pair(b)


def interior(b):
    return pair(b) >= PAIR


def window_kernel(
    w_hbm, own_hbm, opp_hbm, acts_ref, picks_ref, gain_ref, vgain_ref, vout_ref, table_hbm, up_hbm,
    out_ref, scale_ref, val_ref,
    wbuf, rows, own_ref, opp_ref, table, up, tag, picks_all, onehot, order,
    to_sib, from_sib, to_x, from_x, part, ssq, hid, jrow, jsend, arecv, sc_send, sc_recv,
    l_sem, b_sem, w_send, w_recv, e_send, o_send, o_recv, p_send, p_recv, s_send, s_recv, x_send, x_recv,
    a_send, a_recv, c_send, c_recv,
):
    blocks, env, depth, width = wbuf.shape
    rounds, count, model = own_ref.shape
    pieces, steps, envs, lane = jsend.shape[2:]
    share = model // env
    league_me = lax.axis_index("league")
    me = lax.axis_index("env")
    x, core = league_me // 2, league_me % 2
    z, y = me // PAIR, me % PAIR
    sib = x * 2 + (1 - core)
    across = (1 - x) * 2 + core
    diag = (1 - x) * 2 + (1 - core)
    y_peer = z * PAIR + (1 - y)

    barrier = pltpu.get_barrier_semaphore()
    for group in (sib, across, diag):
        pl.semaphore_signal(barrier, inc=1, device_id=(group, me), device_id_type=MESH)
    for d in range(1, env):
        pl.semaphore_signal(barrier, inc=1, device_id=(league_me, (me + d) % env), device_id_type=MESH)

    def piece_copy(kind, b, j):
        start = pl.multiple_of(dest(b, j) * share + (b % 2) * lane, lane)
        cols = pl.ds(j * lane, lane)
        if kind == 0:
            src, dst = w_hbm.at[:, pl.ds(start, lane)], wbuf.at[b, me, :, cols]
        elif kind == 1:
            src, dst = table_hbm.at[:, pl.ds(start, lane)], table.at[b, :, cols]
        else:
            src, dst = up_hbm.at[pl.ds(start, lane)], up.at[b, cols]
        return pltpu.make_async_copy(src, dst, b_sem.at[kind, b, j])

    own_in = pltpu.make_async_copy(own_hbm, own_ref, l_sem.at[0])
    opp_in = pltpu.make_async_copy(opp_hbm, opp_ref, l_sem.at[1])
    for b in range(blocks):
        for j in range(pieces):
            piece_copy(0, b, j).start()
    own_in.start()
    opp_in.start()
    for kind in (1, 2):
        for b in range(blocks):
            for j in range(pieces):
                piece_copy(kind, b, j).start()

    def remote(src, dst, send, recv, group, place):
        return pltpu.make_async_remote_copy(
            src_ref=src, dst_ref=dst, send_sem=send, recv_sem=recv,
            device_id=(group, place), device_id_type=MESH,
        )

    def w_copy(b, line, way, place):
        slot = line * PAIR + y
        return remote(
            wbuf.at[b, slot], wbuf.at[b, slot], w_send.at[b, line, way], w_recv.at[b, slot], league_me, place
        )

    def to_right(b, line):
        return w_copy(b, line, 0, me + PAIR)

    def to_left(b, line):
        return w_copy(b, line, 1, me - PAIR)

    def to_y(b, line):
        return w_copy(b, line, 2, y_peer)

    def w_wait(b, slot):
        remote(
            wbuf.at[b, slot], wbuf.at[b, slot], w_send.at[b, 0, 2], w_recv.at[b, slot], league_me, y_peer
        ).wait_recv()

    def own_sends(b):
        @pl.when(z < LINE - 1)
        def _():
            to_right(b, z).start()

        @pl.when(z > 0)
        def _():
            to_left(b, z).start()

        to_y(b, z).start()

    def by_z(b, line):
        return jnp.logical_or(
            jnp.logical_and(line == z - 1, jnp.logical_or(z == 1, jnp.logical_and(z == LINE - 1, b % BALANCE == 1))),
            jnp.logical_and(line == z + 1, jnp.logical_or(z == LINE - 2, jnp.logical_and(z == 0, b % BALANCE == 1))),
        )

    def other(b, place):
        slot = z * PAIR + 1 - y
        return remote(wbuf.at[b, slot], wbuf.at[b, slot], e_send.at[b], w_recv.at[b, slot], league_me, place)

    def goes_right(b):
        return jnp.logical_or(z == 0, jnp.logical_and(z == LINE - 2, b % BALANCE == 1))

    def goes_left(b):
        return jnp.logical_or(z == LINE - 1, jnp.logical_and(z == 1, b % BALANCE == 1))

    def hop(k):
        b, h = k // (LINE - 1), k % (LINE - 1) + 1
        low, high = z - h, z + h

        @pl.when(low >= 0)
        def _():
            w_wait(b, low * PAIR + y)

            @pl.when(z < LINE - 1)
            def _():
                to_right(b, low).start()

            @pl.when(jnp.logical_not(by_z(b, low)))
            def _():
                to_y(b, low).start()

        @pl.when(high < LINE)
        def _():
            w_wait(b, high * PAIR + y)

            @pl.when(z > 0)
            def _():
                to_left(b, high).start()

            @pl.when(jnp.logical_not(by_z(b, high)))
            def _():
                to_y(b, high).start()

        @pl.when(h == 1)
        def _():
            w_wait(b, z * PAIR + 1 - y)

            @pl.when(goes_right(b))
            def _():
                other(b, me + PAIR).start()

            @pl.when(goes_left(b))
            def _():
                other(b, me - PAIR).start()

        @pl.when(jnp.logical_and(h == 2, b < blocks - AHEAD))
        def _():
            own_sends(b + AHEAD)

    def finish_w_sends(b):
        for line in range(LINE):
            @pl.when(jnp.logical_and(line <= z, z < LINE - 1))
            def _():
                to_right(b, line).wait_send()

            @pl.when(jnp.logical_and(line >= z, z > 0))
            def _():
                to_left(b, line).wait_send()

            @pl.when(jnp.logical_not(by_z(b, line)))
            def _():
                to_y(b, line).wait_send()

        @pl.when(jnp.logical_or(goes_right(b), goes_left(b)))
        def _():
            other(b, y_peer).wait_send()

    def o_copy(r, way):
        if way == 0:
            src, dst, group = opp_hbm.at[r], rows.at[r, ACROSS], across
        elif way == 1:
            src, dst, group = opp_hbm.at[r], rows.at[r, SIB], sib
        else:
            src, dst, group = rows.at[r, ACROSS], rows.at[r, DIAG], sib
        return remote(src, dst, o_send.at[way, r], o_recv.at[way, r], group, me)

    pick_copies = [
        remote(tag, picks_all.at[slot], p_send.at[slot], p_recv.at[slot], group, me)
        for slot, group in ((SIB, sib), (ACROSS, across), (DIAG, diag))
    ]

    def norm(src, dst, tile=64):
        def step(i, _):
            at = pl.ds(pl.multiple_of(i * tile, tile), tile)
            v = src[at, :].astype(F32)
            scale = lax.rsqrt(jnp.mean(v * v, axis=-1, keepdims=True) + 1e-05)
            dst[at, :] = (v * scale * gain_ref[...].astype(F32)).astype(BF16)
            return 0

        lax.fori_loop(0, count // tile, step, 0)

    for b in range(AHEAD):
        for j in range(pieces):
            piece_copy(0, b, j).wait()
    trow = lax.broadcasted_iota(jnp.int32, tag.shape, 0)
    tag[...] = jnp.where(trow == 0, picks_ref[0, 0], picks_ref[0, 1]).astype(F32)
    picks_all[ME] = tag[...]
    pl.semaphore_wait(barrier, 3 + env - 1)
    for copy in pick_copies:
        copy.start()
    for b in range(AHEAD):
        own_sends(b)
    for r in range(rounds):
        o_copy(r, 0).start()
    for r in range(rounds):
        o_copy(r, 1).start()
    for b in range(AHEAD, blocks):
        for j in range(pieces):
            piece_copy(0, b, j).wait()

    row = lax.broadcasted_iota(jnp.int32, (count, count), 0)
    col = lax.broadcasted_iota(jnp.int32, (count, count), 1)
    order[...] = jnp.where(col == (row % envs) * steps + row // envs, 1.0, 0.0).astype(BF16)
    hid[...] = jnp.zeros_like(hid)
    ssq[...] = jnp.zeros_like(ssq)
    own_in.wait()
    norm(own_ref.at[0], rows.at[0, OWN])
    hop(0)
    for r in range(1, rounds):
        norm(own_ref.at[r], rows.at[r, OWN])
    hop(1)
    opp_in.wait()
    for r in range(rounds):
        norm(opp_ref.at[r], rows.at[r, ME])
    hop(2)
    lane_step = lax.broadcasted_iota(jnp.int32, (envs, steps, steps), 2)
    row_step = lax.broadcasted_iota(jnp.int32, (envs, steps, steps), 1)
    for r in range(rounds):
        hot = 0.0
        for side in range(2):
            ids = acts_ref[side, r].astype(F32)
            spread = jnp.where(lane_step == row_step, jnp.broadcast_to(ids[:, None, :], (envs, steps, steps)), 0.0)
            ids = jnp.sum(spread, axis=2, keepdims=True).reshape(count, 1)
            hot = hot + jnp.where(ids == lax.broadcasted_iota(jnp.int32, onehot.shape[1:], 1).astype(F32), 1.0, 0.0)
        onehot[r] = hot.astype(BF16)
    for r in range(rounds):
        o_copy(r, 1).wait_recv()
        norm(rows.at[r, SIB], rows.at[r, SIB])
    for kind in (1, 2):
        for b in range(blocks):
            for j in range(pieces):
                piece_copy(kind, b, j).wait()
    for copy in pick_copies:
        copy.wait_recv()

    def s_copy(b, r, k):
        return remote(to_sib.at[b, k, r], from_sib.at[b, k, r], s_send.at[b, r, k], s_recv.at[b, r, k], sib, me)

    def x_copy(b, r):
        return remote(to_x.at[b, r], from_x.at[b, r], x_send.at[b, r], x_recv.at[b, r], across, me)

    mine = league_me.astype(F32)

    def column(b, j):
        return pl.ds(pl.multiple_of(dest(b, j) * share + (b % 2) * lane, lane), lane)

    def arrive(r):
        o_copy(r, 0).wait_recv()
        o_copy(r, 2).start()
        o_copy(r, 2).wait_recv()
        norm(rows.at[r, DIAG], rows.at[r, DIAG])
        o_copy(r, 2).wait_send()
        norm(rows.at[r, ACROSS], rows.at[r, ACROSS])

    def ready(b):
        for line in range(LINE):
            @pl.when(line != z)
            def _():
                w_wait(b, line * PAIR + (1 - y))

    def dot(b, r, slot):
        return jnp.dot(rows[r, slot], wbuf[b].reshape(env * depth, width), preferred_element_type=F32)

    def served(b, r, slot):
        chosen = jnp.where(r == 0, picks_all[slot, 0:1, :], picks_all[slot, 1:2, :])[:, :1]
        return dot(b, r, slot) * jnp.where(chosen == mine, 1.0, 0.0)

    def for_diag(b, r):
        to_sib[b, 0, r] = served(b, r, DIAG).astype(BF16)
        s_copy(b, r, 0).start()

    def for_across(b, r):
        to_x[b, r] = served(b, r, ACROSS).astype(BF16)
        s_copy(b, r, 0).wait_recv()
        to_x[b, r] = to_x[b, r] + from_sib[b, 0, r]
        x_copy(b, r).start()

    def here(b, r):
        to_sib[b, 1, r] = served(b, r, SIB).astype(BF16)
        s_copy(b, r, 1).start()
        part[b, r] = jnp.dot(onehot[r], table[b], preferred_element_type=F32)
        part[b, r] += dot(b, r, OWN)
        part[b, r] += served(b, r, ME)
        for j in range(pieces):
            cols = pl.ds(j * lane, lane)
            at = column(b, j)
            part[b, r, :, cols] += own_ref[r, :, at].astype(F32) + opp_ref[r, :, at].astype(F32)

    def a_copy(b, r, j):
        target = dest(b, j)
        return remote(
            jsend.at[b, r, j], arecv.at[r, b % 2, me], a_send.at[b, r, j], a_recv.at[r, b % 2, me],
            league_me, target,
        )

    def a_each(b, r, do, near=True, far=True):
        for j in range(pieces):
            crosses = dest(b, j) % PAIR != y

            @pl.when(jnp.logical_and(dest(b, j) != me, jnp.where(crosses, far, near)))
            def _():
                do(j)

    tile = 64

    def finish(b, r, now):
        s_copy(b, r, 1).wait_recv()
        x_copy(b, r).wait_recv()
        gains = jnp.concatenate([vgain_ref[:, column(b, j)] for j in range(pieces)], axis=1).astype(F32)

        def joint_tile(i, _):
            at = pl.ds(pl.multiple_of(i * tile, tile), tile)
            v = part[b, r, at, :] + from_sib[b, 1, r, at, :].astype(F32) + from_x[b, r, at, :].astype(F32)
            ssq[r, at, :] += jnp.broadcast_to(jnp.sum(v * v, axis=-1, keepdims=True), (tile, lane))
            jrow[r, at, :] = (v * gains).astype(BF16)
            return 0

        lax.fori_loop(0, count // tile, joint_tile, 0)
        moved = jnp.dot(order[...], jrow[r], preferred_element_type=F32).astype(BF16)
        for j in range(pieces):
            jsend[b, r, j] = moved[:, j * lane:(j + 1) * lane].reshape(steps, envs, lane)
        a_each(b, r, lambda j: a_copy(b, r, j).start(), near=jnp.logical_or(now, interior(b)), far=now)
        for j in range(pieces):
            @pl.when(dest(b, j) == me)
            def _():
                arecv[r, b % 2, me] = jsend[b, r, j]
        hid[r] += jnp.dot(jrow[r], up[b], preferred_element_type=F32)

    def release(b, r):
        a_each(b, r, lambda j: a_copy(b, r, j).start(), near=jnp.logical_not(interior(b)))

    def choose_at(i, values, start, stop):
        if stop - start == 1:
            return jnp.int32(values[start])
        middle = (start + stop) // 2
        return jnp.where(i < middle, choose_at(i, values, start, middle), choose_at(i, values, middle, stop))

    def act(i, _):
        word = choose_at(lax.div(i, 3), PLAN, 0, len(PLAN))
        turn = lax.rem(i, 3)
        code = lax.rem(jnp.where(turn == 0, word, jnp.where(turn == 1, lax.div(word, 1024), lax.div(word, 1024 * 1024))), 1024)
        kind, arg = lax.div(code, 32), lax.rem(code, 32)
        b, r = lax.div(arg, rounds), lax.rem(arg, rounds)
        for k, do in enumerate((
            lambda: hop(arg), lambda: arrive(arg), lambda: ready(arg), lambda: for_diag(b, r),
            lambda: for_across(b, r), lambda: here(b, r), lambda: finish(b, r, kind == 6), None,
            lambda: release(b, r),
        )):
            if do is not None:
                pl.when(jnp.logical_or(kind == 6, kind == 7) if k == 6 else kind == k)(do)

        return 0

    lax.fori_loop(0, 3 * len(PLAN), act, 0)

    def w_sent(b, _):
        finish_w_sends(b)
        return 0

    lax.fori_loop(0, blocks, w_sent, 0)
    row_env = lax.broadcasted_iota(jnp.int32, (count, lane), 0) // steps
    at_lane = lax.broadcasted_iota(jnp.int32, (count, lane), 1)

    def c_copy(r, d):
        return remote(
            sc_send.at[r], sc_recv.at[r, me], c_send.at[r, d], c_recv.at[r, me], league_me, (me + d) % env
        )

    for r in range(rounds):
        scale = lax.rsqrt(ssq[r] * (1.0 / model) + 1e-05)
        ssq[r] = scale
        placed = jnp.where(at_lane == me * envs + row_env, scale, 0.0)
        sc_send[r] = jnp.sum(placed.reshape(envs, steps, lane), axis=0)
        for d in range(1, env):
            c_copy(r, d).start()
        sc_recv[r, me] = sc_send[r]

    row_step = lax.broadcasted_iota(jnp.int32, (count, lane), 0) % steps
    for r in range(rounds):
        hidden = hid[r] * ssq[r][:, :1]
        hidden = (hidden / (1.0 + jnp.exp(-hidden))).astype(BF16).astype(F32)
        value = jnp.sum(hidden * vout_ref[...].astype(F32), axis=-1, keepdims=True)
        spread = jnp.where(at_lane == row_step, value, 0.0)
        val_ref[r] = jnp.sum(spread.reshape(envs, steps, lane), axis=1)[:, :steps]

    for half in range(2):
        for r in range(rounds):
            for d in range(1, env):
                peer = (me + d) % env
                remote(
                    jsend.at[0, r, 0], arecv.at[r, half, peer], a_send.at[0, r, 0], a_recv.at[r, half, peer],
                    league_me, peer,
                ).wait_recv()

            def turn(i, _):
                for t in range(TURN):
                    piece = arecv[r, half, :, i * TURN + t].reshape(env * envs, lane)
                    out_ref[r, i * TURN + t, half * lane:(half + 1) * lane, :] = piece.T
                return 0

            lax.fori_loop(0, steps // TURN, turn, 0)
    for r in range(rounds):
        total = sc_recv[r, me]
        for d in range(1, env):
            peer = (me + d) % env
            remote(
                sc_send.at[r], sc_recv.at[r, peer], c_send.at[r, d], c_recv.at[r, peer], league_me, peer
            ).wait_recv()
            total = total + sc_recv[r, peer]
        scale_ref[r] = total

    def sent(q, _):
        b, r = q // rounds, q % rounds
        s_copy(b, r, 0).wait_send()
        s_copy(b, r, 1).wait_send()
        x_copy(b, r).wait_send()
        a_each(b, r, lambda j: a_copy(b, r, j).wait_send())
        return 0

    lax.fori_loop(0, blocks * rounds, sent, 0)
    for copy in pick_copies:
        copy.wait_send()
    for r in range(rounds):
        o_copy(r, 0).wait_send()
        o_copy(r, 1).wait_send()
        for d in range(1, env):
            c_copy(r, d).wait_send()


def fused(
    obs_own,
    obs_opp,
    actions,
    opponent_picks,
    policy_weight,
    policy_gain,
    action_table,
    value_gain,
    value_up,
    value_out,
):
    rounds, envs, steps, model = obs_own.shape[1:]
    count = envs * steps
    env = lax.axis_size("env")
    depth = policy_weight.shape[1]
    width = model // BLOCKS
    share = model // env
    lane = share // 2
    pieces = width // lane
    hidden = value_up.shape[1]
    choices = action_table.shape[0]
    vmem = pl.BlockSpec(memory_space=pltpu.VMEM)
    smem = pl.BlockSpec(memory_space=pltpu.SMEM)
    hbm = pl.BlockSpec(memory_space=pl.ANY)
    dma = pltpu.SemaphoreType.DMA
    turned, scales, val = pl.pallas_call(
        window_kernel,
        out_shape=(
            jax.ShapeDtypeStruct((rounds, steps, share, env * envs), BF16),
            jax.ShapeDtypeStruct((rounds, steps, lane), F32),
            jax.ShapeDtypeStruct((rounds, envs, steps), F32),
        ),
        in_specs=[hbm, hbm, hbm, vmem, smem, vmem, vmem, vmem, hbm, hbm],
        out_specs=(vmem, vmem, vmem),
        scratch_shapes=[
            pltpu.VMEM((BLOCKS, env, depth, width), BF16),
            pltpu.VMEM((rounds, 5, count, model), BF16),
            pltpu.VMEM((rounds, count, model), BF16),
            pltpu.VMEM((rounds, count, model), BF16),
            pltpu.VMEM((BLOCKS, choices, width), BF16),
            pltpu.VMEM((BLOCKS, width, hidden), BF16),
            pltpu.VMEM((8, 128), F32),
            pltpu.VMEM((5, 8, 128), F32),
            pltpu.VMEM((rounds, count, choices), BF16),
            pltpu.VMEM((count, count), BF16),
            pltpu.VMEM((BLOCKS, 2, rounds, count, width), BF16),
            pltpu.VMEM((BLOCKS, 2, rounds, count, width), BF16),
            pltpu.VMEM((BLOCKS, rounds, count, width), BF16),
            pltpu.VMEM((BLOCKS, rounds, count, width), BF16),
            pltpu.VMEM((BLOCKS, rounds, count, width), F32),
            pltpu.VMEM((rounds, count, lane), F32),
            pltpu.VMEM((rounds, count, hidden), F32),
            pltpu.VMEM((rounds, count, width), BF16),
            pltpu.VMEM((BLOCKS, rounds, pieces, steps, envs, lane), BF16),
            pltpu.VMEM((rounds, 2, env, steps, envs, lane), BF16),
            pltpu.VMEM((rounds, steps, lane), F32),
            pltpu.VMEM((rounds, env, steps, lane), F32),
            dma((2,)),
            dma((3, BLOCKS, pieces)),
            dma((BLOCKS, LINE, 3)),
            dma((BLOCKS, env)),
            dma((BLOCKS,)),
            dma((3, rounds)),
            dma((3, rounds)),
            dma((5,)),
            dma((5,)),
            dma((BLOCKS, rounds, 2)),
            dma((BLOCKS, rounds, 2)),
            dma((BLOCKS, rounds)),
            dma((BLOCKS, rounds)),
            dma((BLOCKS, rounds, pieces)),
            dma((rounds, 2, env)),
            dma((rounds, env)),
            dma((rounds, env)),
        ],
        compiler_params=pltpu.CompilerParams(
            collective_id=0, has_side_effects=True, vmem_limit_bytes=62 * MIB
        ),
    )(
        policy_weight[0],
        obs_own[0].reshape(rounds, count, model),
        obs_opp[0].reshape(rounds, count, model),
        actions[0],
        opponent_picks,
        policy_gain,
        value_gain[None],
        value_out[None],
        action_table,
        value_up,
    )
    out = (turned.astype(F32) * scales[:, :, None, :]).astype(BF16)
    return (out[None], val[None])


def solution(mesh):
    in_specs = (
        P("league", None, "env", None, None),
        P("league", None, "env", None, None),
        P("league", None, None, "env", None),
        P("league", None),
        P("league", "env", None),
        P("league", None),
        P(),
        P(),
        P(),
        P(),
    )
    out_specs = (P("league", None, None, "env", None), P("league", None, "env", None))
    body = fused if mesh.shape["env"] == LINE * PAIR else local
    return jax.shard_map(body, mesh=mesh, in_specs=in_specs, out_specs=out_specs, check_vma=False)
```

```python
import functools

import jax
import jax.numpy as jnp
from jax import lax
from jax.experimental import pallas as pl
from jax.experimental.pallas import tpu as pltpu
from jax.sharding import PartitionSpec as P

F32 = jnp.float32
BF16 = jnp.bfloat16
BLOCKS = 8
LINE = 4
PAIR = 2
MIB = 1 << 20
OWN, ME, SIB, ACROSS, DIAG = range(5)
MESH = pl.DeviceIdType.MESH


def rms_norm(inputs, gain):
    scale = lax.rsqrt(jnp.mean(inputs * inputs, axis=-1, keepdims=True) + 1e-05)
    return inputs * scale * gain.astype(jnp.float32)


def local(
    obs_own,
    obs_opp,
    actions,
    opponent_picks,
    policy_weight,
    policy_gain,
    action_table,
    value_gain,
    value_up,
    value_out,
):
    round_count = obs_own.shape[1]
    env_count = obs_own.shape[2]
    step_count = obs_own.shape[3]
    model_width = obs_own.shape[4]
    row_count = env_count * step_count
    weight_shard = policy_weight[0]
    own_gain = policy_gain[0]
    group_count = lax.axis_size("league")
    my_group = lax.axis_index("league")
    own_inputs = obs_own[0].reshape(round_count * row_count, model_width).astype(jnp.float32)
    own_normed = rms_norm(own_inputs, own_gain).astype(jnp.bfloat16)
    own_whole = lax.all_gather(weight_shard, "env", axis=0, tiled=True)
    own_state = own_inputs + jnp.dot(own_normed, own_whole, preferred_element_type=jnp.float32)
    every_pick = lax.all_gather(opponent_picks, "league", axis=0, tiled=True)
    action_range = jnp.arange(action_table.shape[0], dtype=jnp.int32)
    traj_list = []
    value_list = []
    for round_index in range(round_count):
        opp_raw = obs_opp[0, round_index].reshape(row_count, model_width)
        opp_inputs = opp_raw.astype(jnp.float32)
        all_rows = lax.all_gather(opp_raw, "league", axis=0, tiled=True)
        all_normed = rms_norm(all_rows.astype(jnp.float32), own_gain).astype(jnp.bfloat16)
        products = jnp.dot(all_normed, own_whole, preferred_element_type=jnp.float32)
        served = (every_pick[:, round_index] == my_group).astype(jnp.float32)
        products = (
            products.reshape(group_count, row_count, model_width) * served[:, None, None]
        ).astype(jnp.bfloat16)
        answers = lax.all_to_all(products, "league", split_axis=0, concat_axis=0, tiled=True)
        opp_state = opp_inputs + jnp.sum(answers.astype(jnp.float32), axis=0)
        own_ids = actions[0, 0, round_index].reshape(row_count)
        opp_ids = actions[0, 1, round_index].reshape(row_count)
        onehot = (own_ids[:, None] == action_range[None, :]).astype(jnp.bfloat16) + (
            opp_ids[:, None] == action_range[None, :]
        ).astype(jnp.bfloat16)
        action_sum = jnp.dot(onehot, action_table, preferred_element_type=jnp.float32)
        round_state = lax.dynamic_slice_in_dim(own_state, round_index * row_count, row_count, 0)
        joint_sum = round_state + opp_state + action_sum
        joint_row = rms_norm(joint_sum, value_gain).astype(jnp.bfloat16)
        value_hidden = jax.nn.silu(
            jnp.dot(joint_row, value_up, preferred_element_type=jnp.float32)
        ).astype(jnp.bfloat16)
        value_est = jnp.dot(value_hidden, value_out, preferred_element_type=jnp.float32)
        value_list.append(value_est.reshape(env_count, step_count))
        time_block = joint_row.reshape(env_count, step_count, model_width).transpose(1, 2, 0)
        traj_list.append(lax.all_to_all(time_block, "env", split_axis=1, concat_axis=2, tiled=True))
    learner_rows = jnp.stack(traj_list)
    values = jnp.stack(value_list)
    return (learner_rows[None], values[None])


PLAN = (
    167837699, 5247137, 169935878, 8555527, 102858784, 136445961, 104925194, 173026468,
    13643908, 107023374, 175127718, 17842310, 103908385, 108106770, 135372868, 20030595,
    142744709, 21112032, 239247586, 241345557, 111219734, 24291435, 272894208, 145893638,
    204647617, 113318085, 208842861, 181548172, 74654920, 211926126, 150091950, 214117551,
    217266381,
)
TURN = 8
FIRST = 2
BALANCE = 2
AHEAD = 2


def pair(b):
    return (b // 2 + FIRST) % LINE


def dest(b, j):
    return pair(b) if j == 0 else LINE * PAIR - 1 - pair(b)


def interior(b):
    return pair(b) >= PAIR


def window_kernel(
    w_hbm, own_hbm, opp_hbm, acts_ref, picks_ref, gain_ref, both_ref, table_hbm, up_hbm,
    out_ref, scale_ref, val_ref,
    wbuf, rows, own_ref, opp_ref, table, up, tag, picks_all, onehot, order,
    to_sib, from_sib, to_x, from_x, part, ssq, hid, jrow, jsend, arecv, sc_send, sc_recv,
    l_sem, b_sem, w_send, w_recv, e_send, o_send, o_recv, p_send, p_recv, s_send, s_recv, x_send, x_recv,
    a_send, a_recv, c_send, c_recv,
):
    blocks, env, depth, width = wbuf.shape
    rounds, count, model = own_ref.shape
    pieces, steps, envs, lane = jsend.shape[2:]
    share = model // env
    vgain_ref = both_ref.at[:, 0:model]
    vout_ref = both_ref.at[:, model:]
    league_me = lax.axis_index("league")
    me = lax.axis_index("env")
    x, core = league_me // 2, league_me % 2
    z, y = me // PAIR, me % PAIR
    sib = x * 2 + (1 - core)
    across = (1 - x) * 2 + core
    diag = (1 - x) * 2 + (1 - core)
    y_peer = z * PAIR + (1 - y)

    barrier = pltpu.get_barrier_semaphore()
    for group in (sib, across, diag):
        pl.semaphore_signal(barrier, inc=1, device_id=(group, me), device_id_type=MESH)
    for d in range(1, env):
        pl.semaphore_signal(barrier, inc=1, device_id=(league_me, (me + d) % env), device_id_type=MESH)

    def piece_copy(kind, b, j):
        start = pl.multiple_of(dest(b, j) * share + (b % 2) * lane, lane)
        cols = pl.ds(j * lane, lane)
        if kind == 0:
            src, dst = w_hbm.at[:, pl.ds(start, lane)], wbuf.at[b, me, :, cols]
        elif kind == 1:
            src, dst = table_hbm.at[:, pl.ds(start, lane)], table.at[b, :, cols]
        else:
            src, dst = up_hbm.at[pl.ds(start, lane)], up.at[b, cols]
        return pltpu.make_async_copy(src, dst, b_sem.at[kind, b, j])

    own_in = pltpu.make_async_copy(own_hbm, own_ref, l_sem.at[0])
    opp_in = pltpu.make_async_copy(opp_hbm, opp_ref, l_sem.at[1])
    for b in range(blocks):
        for j in range(pieces):
            piece_copy(0, b, j).start()
    own_in.start()
    opp_in.start()
    for kind in (1, 2):
        for b in range(blocks):
            for j in range(pieces):
                piece_copy(kind, b, j).start()

    def remote(src, dst, send, recv, group, place):
        return pltpu.make_async_remote_copy(
            src_ref=src, dst_ref=dst, send_sem=send, recv_sem=recv,
            device_id=(group, place), device_id_type=MESH,
        )

    def w_copy(b, line, way, place):
        slot = line * PAIR + y
        return remote(
            wbuf.at[b, slot], wbuf.at[b, slot], w_send.at[b, line, way], w_recv.at[b, slot], league_me, place
        )

    def to_right(b, line):
        return w_copy(b, line, 0, me + PAIR)

    def to_left(b, line):
        return w_copy(b, line, 1, me - PAIR)

    def to_y(b, line):
        return w_copy(b, line, 2, y_peer)

    def w_wait(b, slot):
        remote(
            wbuf.at[b, slot], wbuf.at[b, slot], w_send.at[b, 0, 2], w_recv.at[b, slot], league_me, y_peer
        ).wait_recv()

    def own_sends(b):
        @pl.when(z < LINE - 1)
        def _():
            to_right(b, z).start()

        @pl.when(z > 0)
        def _():
            to_left(b, z).start()

        to_y(b, z).start()

    def by_z(b, line):
        return jnp.logical_or(
            jnp.logical_and(line == z - 1, jnp.logical_or(z == 1, jnp.logical_and(z == LINE - 1, b % BALANCE == 1))),
            jnp.logical_and(line == z + 1, jnp.logical_or(z == LINE - 2, jnp.logical_and(z == 0, b % BALANCE == 1))),
        )

    def other(b, place):
        slot = z * PAIR + 1 - y
        return remote(wbuf.at[b, slot], wbuf.at[b, slot], e_send.at[b], w_recv.at[b, slot], league_me, place)

    def goes_right(b):
        return jnp.logical_or(z == 0, jnp.logical_and(z == LINE - 2, b % BALANCE == 1))

    def goes_left(b):
        return jnp.logical_or(z == LINE - 1, jnp.logical_and(z == 1, b % BALANCE == 1))

    def hop(k):
        b, h = k // (LINE - 1), k % (LINE - 1) + 1
        low, high = z - h, z + h

        @pl.when(low >= 0)
        def _():
            w_wait(b, low * PAIR + y)

            @pl.when(z < LINE - 1)
            def _():
                to_right(b, low).start()

            @pl.when(jnp.logical_not(by_z(b, low)))
            def _():
                to_y(b, low).start()

        @pl.when(high < LINE)
        def _():
            w_wait(b, high * PAIR + y)

            @pl.when(z > 0)
            def _():
                to_left(b, high).start()

            @pl.when(jnp.logical_not(by_z(b, high)))
            def _():
                to_y(b, high).start()

        @pl.when(h == 1)
        def _():
            w_wait(b, z * PAIR + 1 - y)

            @pl.when(goes_right(b))
            def _():
                other(b, me + PAIR).start()

            @pl.when(goes_left(b))
            def _():
                other(b, me - PAIR).start()

        @pl.when(jnp.logical_and(h == 2, b < blocks - AHEAD))
        def _():
            own_sends(b + AHEAD)

    def finish_w_sends(b):
        for line in range(LINE):
            @pl.when(jnp.logical_and(line <= z, z < LINE - 1))
            def _():
                to_right(b, line).wait_send()

            @pl.when(jnp.logical_and(line >= z, z > 0))
            def _():
                to_left(b, line).wait_send()

            @pl.when(jnp.logical_not(by_z(b, line)))
            def _():
                to_y(b, line).wait_send()

        @pl.when(jnp.logical_or(goes_right(b), goes_left(b)))
        def _():
            other(b, y_peer).wait_send()

    def o_copy(r, way):
        if way == 0:
            src, dst, group = opp_hbm.at[r], rows.at[r, ACROSS], across
        elif way == 1:
            src, dst, group = opp_hbm.at[r], rows.at[r, SIB], sib
        else:
            src, dst, group = rows.at[r, ACROSS], rows.at[r, DIAG], sib
        return remote(src, dst, o_send.at[way, r], o_recv.at[way, r], group, me)

    pick_copies = [
        remote(tag, picks_all.at[slot], p_send.at[slot], p_recv.at[slot], group, me)
        for slot, group in ((SIB, sib), (ACROSS, across), (DIAG, diag))
    ]

    def norm(src, dst, tile=64):
        def step(i, _):
            at = pl.ds(pl.multiple_of(i * tile, tile), tile)
            v = src[at, :].astype(F32)
            scale = lax.rsqrt(jnp.mean(v * v, axis=-1, keepdims=True) + 1e-05)
            dst[at, :] = (v * scale * gain_ref[...].astype(F32)).astype(BF16)
            return 0

        lax.fori_loop(0, count // tile, step, 0)

    for b in range(AHEAD):
        for j in range(pieces):
            piece_copy(0, b, j).wait()
    trow = lax.broadcasted_iota(jnp.int32, tag.shape, 0)
    tag[...] = jnp.where(trow == 0, picks_ref[0, 0], picks_ref[0, 1]).astype(F32)
    picks_all[ME] = tag[...]
    pl.semaphore_wait(barrier, 3 + env - 1)
    for copy in pick_copies:
        copy.start()
    for b in range(AHEAD):
        own_sends(b)
    for r in range(rounds):
        o_copy(r, 0).start()
    for r in range(rounds):
        o_copy(r, 1).start()
    for b in range(AHEAD, blocks):
        for j in range(pieces):
            piece_copy(0, b, j).wait()

    row = lax.broadcasted_iota(jnp.int32, (count, count), 0)
    col = lax.broadcasted_iota(jnp.int32, (count, count), 1)
    order[...] = jnp.where(col == (row % envs) * steps + row // envs, 1.0, 0.0).astype(BF16)
    hid[...] = jnp.zeros_like(hid)
    ssq[...] = jnp.zeros_like(ssq)
    own_in.wait()
    norm(own_ref.at[0], rows.at[0, OWN])
    hop(0)
    for r in range(1, rounds):
        norm(own_ref.at[r], rows.at[r, OWN])
    hop(1)
    opp_in.wait()
    for r in range(rounds):
        norm(opp_ref.at[r], rows.at[r, ME])
    hop(2)
    lane_step = lax.broadcasted_iota(jnp.int32, (envs, steps, steps), 2)
    row_step = lax.broadcasted_iota(jnp.int32, (envs, steps, steps), 1)
    for r in range(rounds):
        hot = 0.0
        for side in range(2):
            ids = acts_ref[side, r].astype(F32)
            spread = jnp.where(lane_step == row_step, jnp.broadcast_to(ids[:, None, :], (envs, steps, steps)), 0.0)
            ids = jnp.sum(spread, axis=2, keepdims=True).reshape(count, 1)
            hot = hot + jnp.where(ids == lax.broadcasted_iota(jnp.int32, onehot.shape[1:], 1).astype(F32), 1.0, 0.0)
        onehot[r] = hot.astype(BF16)
    for r in range(rounds):
        o_copy(r, 1).wait_recv()
        norm(rows.at[r, SIB], rows.at[r, SIB])
    for kind in (1, 2):
        for b in range(blocks):
            for j in range(pieces):
                piece_copy(kind, b, j).wait()
    for copy in pick_copies:
        copy.wait_recv()

    def s_copy(b, r, k):
        return remote(to_sib.at[b, k, r], from_sib.at[b, k, r], s_send.at[b, r, k], s_recv.at[b, r, k], sib, me)

    def x_copy(b, r):
        return remote(to_x.at[b, r], from_x.at[b, r], x_send.at[b, r], x_recv.at[b, r], across, me)

    mine = league_me.astype(F32)

    def column(b, j):
        return pl.ds(pl.multiple_of(dest(b, j) * share + (b % 2) * lane, lane), lane)

    def arrive(r):
        o_copy(r, 0).wait_recv()
        o_copy(r, 2).start()
        o_copy(r, 2).wait_recv()
        norm(rows.at[r, DIAG], rows.at[r, DIAG])
        o_copy(r, 2).wait_send()
        norm(rows.at[r, ACROSS], rows.at[r, ACROSS])

    def ready(b):
        for line in range(LINE):
            @pl.when(line != z)
            def _():
                w_wait(b, line * PAIR + (1 - y))

    def dot(b, r, slot):
        return jnp.dot(rows[r, slot], wbuf[b].reshape(env * depth, width), preferred_element_type=F32)

    def served(b, r, slot):
        chosen = jnp.where(r == 0, picks_all[slot, 0:1, :], picks_all[slot, 1:2, :])[:, :1]
        return dot(b, r, slot) * jnp.where(chosen == mine, 1.0, 0.0)

    def for_diag(b, r):
        to_sib[b, 0, r] = served(b, r, DIAG).astype(BF16)
        s_copy(b, r, 0).start()

    def for_across(b, r):
        to_x[b, r] = served(b, r, ACROSS).astype(BF16)
        s_copy(b, r, 0).wait_recv()
        to_x[b, r] = to_x[b, r] + from_sib[b, 0, r]
        x_copy(b, r).start()

    def here(b, r):
        to_sib[b, 1, r] = served(b, r, SIB).astype(BF16)
        s_copy(b, r, 1).start()
        part[b, r] = jnp.dot(onehot[r], table[b], preferred_element_type=F32)
        part[b, r] += dot(b, r, OWN)
        part[b, r] += served(b, r, ME)
        for j in range(pieces):
            cols = pl.ds(j * lane, lane)
            at = column(b, j)
            part[b, r, :, cols] += own_ref[r, :, at].astype(F32) + opp_ref[r, :, at].astype(F32)

    def a_copy(b, r, j):
        target = dest(b, j)
        return remote(
            jsend.at[b, r, j], arecv.at[r, b % 2, me], a_send.at[b, r, j], a_recv.at[r, b % 2, me],
            league_me, target,
        )

    def a_each(b, r, do, near=True, far=True):
        for j in range(pieces):
            crosses = dest(b, j) % PAIR != y

            @pl.when(jnp.logical_and(dest(b, j) != me, jnp.where(crosses, far, near)))
            def _():
                do(j)

    tile = 64

    def finish(b, r, now):
        s_copy(b, r, 1).wait_recv()
        x_copy(b, r).wait_recv()
        gains = jnp.concatenate([vgain_ref[:, column(b, j)] for j in range(pieces)], axis=1).astype(F32)

        def joint_tile(i, _):
            at = pl.ds(pl.multiple_of(i * tile, tile), tile)
            v = part[b, r, at, :] + from_sib[b, 1, r, at, :].astype(F32) + from_x[b, r, at, :].astype(F32)
            ssq[r, at, :] += jnp.broadcast_to(jnp.sum(v * v, axis=-1, keepdims=True), (tile, lane))
            jrow[r, at, :] = (v * gains).astype(BF16)
            return 0

        lax.fori_loop(0, count // tile, joint_tile, 0)
        moved = jnp.dot(order[...], jrow[r], preferred_element_type=F32).astype(BF16)
        for j in range(pieces):
            jsend[b, r, j] = moved[:, j * lane:(j + 1) * lane].reshape(steps, envs, lane)
        a_each(b, r, lambda j: a_copy(b, r, j).start(), near=jnp.logical_or(now, interior(b)), far=now)
        for j in range(pieces):
            @pl.when(dest(b, j) == me)
            def _():
                arecv[r, b % 2, me] = jsend[b, r, j]
        hid[r] += jnp.dot(jrow[r], up[b], preferred_element_type=F32)

    def release(b, r):
        a_each(b, r, lambda j: a_copy(b, r, j).start(), near=jnp.logical_not(interior(b)))

    def choose_at(i, values, start, stop):
        if stop - start == 1:
            return jnp.int32(values[start])
        middle = (start + stop) // 2
        return jnp.where(i < middle, choose_at(i, values, start, middle), choose_at(i, values, middle, stop))

    def act(i, _):
        word = choose_at(lax.div(i, 3), PLAN, 0, len(PLAN))
        turn = lax.rem(i, 3)
        code = lax.rem(jnp.where(turn == 0, word, jnp.where(turn == 1, lax.div(word, 1024), lax.div(word, 1024 * 1024))), 1024)
        kind, arg = lax.div(code, 32), lax.rem(code, 32)
        b, r = lax.div(arg, rounds), lax.rem(arg, rounds)
        for k, do in enumerate((
            lambda: hop(arg), lambda: arrive(arg), lambda: ready(arg), lambda: for_diag(b, r),
            lambda: for_across(b, r), lambda: here(b, r), lambda: finish(b, r, kind == 6), None,
            lambda: release(b, r),
        )):
            if do is not None:
                pl.when(jnp.logical_or(kind == 6, kind == 7) if k == 6 else kind == k)(do)

        return 0

    lax.fori_loop(0, 3 * len(PLAN), act, 0)

    def w_sent(b, _):
        finish_w_sends(b)
        return 0

    lax.fori_loop(0, blocks, w_sent, 0)
    row_env = lax.broadcasted_iota(jnp.int32, (count, lane), 0) // steps
    at_lane = lax.broadcasted_iota(jnp.int32, (count, lane), 1)

    def c_copy(r, d):
        return remote(
            sc_send.at[r], sc_recv.at[r, me], c_send.at[r, d], c_recv.at[r, me], league_me, (me + d) % env
        )

    for r in range(rounds):
        scale = lax.rsqrt(ssq[r] * (1.0 / model) + 1e-05)
        ssq[r] = scale
        placed = jnp.where(at_lane == me * envs + row_env, scale, 0.0)
        sc_send[r] = jnp.sum(placed.reshape(envs, steps, lane), axis=0)
        for d in range(1, env):
            c_copy(r, d).start()
        sc_recv[r, me] = sc_send[r]

    row_step = lax.broadcasted_iota(jnp.int32, (count, lane), 0) % steps
    for r in range(rounds):
        hidden = hid[r] * ssq[r][:, :1]
        hidden = (hidden / (1.0 + jnp.exp(-hidden))).astype(BF16).astype(F32)
        value = jnp.sum(hidden * vout_ref[...].astype(F32), axis=-1, keepdims=True)
        spread = jnp.where(at_lane == row_step, value, 0.0)
        val_ref[r] = jnp.sum(spread.reshape(envs, steps, lane), axis=1)[:, :steps]

    for half in range(2):
        for r in range(rounds):
            for d in range(1, env):
                peer = (me + d) % env
                remote(
                    jsend.at[0, r, 0], arecv.at[r, half, peer], a_send.at[0, r, 0], a_recv.at[r, half, peer],
                    league_me, peer,
                ).wait_recv()

            def turn(i, _):
                for t in range(TURN):
                    piece = arecv[r, half, :, i * TURN + t].reshape(env * envs, lane)
                    out_ref[r, i * TURN + t, half * lane:(half + 1) * lane, :] = piece.T
                return 0

            lax.fori_loop(0, steps // TURN, turn, 0)
    for r in range(rounds):
        total = sc_recv[r, me]
        for d in range(1, env):
            peer = (me + d) % env
            remote(
                sc_send.at[r], sc_recv.at[r, peer], c_send.at[r, d], c_recv.at[r, peer], league_me, peer
            ).wait_recv()
            total = total + sc_recv[r, peer]
        scale_ref[r] = total

    def sent(q, _):
        b, r = q // rounds, q % rounds
        s_copy(b, r, 0).wait_send()
        s_copy(b, r, 1).wait_send()
        x_copy(b, r).wait_send()
        a_each(b, r, lambda j: a_copy(b, r, j).wait_send())
        return 0

    lax.fori_loop(0, blocks * rounds, sent, 0)
    for copy in pick_copies:
        copy.wait_send()
    for r in range(rounds):
        o_copy(r, 0).wait_send()
        o_copy(r, 1).wait_send()
        for d in range(1, env):
            c_copy(r, d).wait_send()


def fused(
    obs_own,
    obs_opp,
    actions,
    opponent_picks,
    policy_weight,
    policy_gain,
    action_table,
    value_gain,
    value_up,
    value_out,
):
    rounds, envs, steps, model = obs_own.shape[1:]
    count = envs * steps
    env = lax.axis_size("env")
    depth = policy_weight.shape[1]
    width = model // BLOCKS
    share = model // env
    lane = share // 2
    pieces = width // lane
    hidden = value_up.shape[1]
    choices = action_table.shape[0]
    vmem = pl.BlockSpec(memory_space=pltpu.VMEM)
    smem = pl.BlockSpec(memory_space=pltpu.SMEM)
    hbm = pl.BlockSpec(memory_space=pl.ANY)
    dma = pltpu.SemaphoreType.DMA
    turned, scales, val = pl.pallas_call(
        window_kernel,
        out_shape=(
            jax.ShapeDtypeStruct((rounds, steps, share, env * envs), BF16),
            jax.ShapeDtypeStruct((rounds, steps, lane), F32),
            jax.ShapeDtypeStruct((rounds, envs, steps), F32),
        ),
        in_specs=[hbm, hbm, hbm, vmem, smem, vmem, vmem, hbm, hbm],
        out_specs=(vmem, vmem, vmem),
        scratch_shapes=[
            pltpu.VMEM((BLOCKS, env, depth, width), BF16),
            pltpu.VMEM((rounds, 5, count, model), BF16),
            pltpu.VMEM((rounds, count, model), BF16),
            pltpu.VMEM((rounds, count, model), BF16),
            pltpu.VMEM((BLOCKS, choices, width), BF16),
            pltpu.VMEM((BLOCKS, width, hidden), BF16),
            pltpu.VMEM((8, 128), F32),
            pltpu.VMEM((5, 8, 128), F32),
            pltpu.VMEM((rounds, count, choices), BF16),
            pltpu.VMEM((count, count), BF16),
            pltpu.VMEM((BLOCKS, 2, rounds, count, width), BF16),
            pltpu.VMEM((BLOCKS, 2, rounds, count, width), BF16),
            pltpu.VMEM((BLOCKS, rounds, count, width), BF16),
            pltpu.VMEM((BLOCKS, rounds, count, width), BF16),
            pltpu.VMEM((BLOCKS, rounds, count, width), F32),
            pltpu.VMEM((rounds, count, lane), F32),
            pltpu.VMEM((rounds, count, hidden), F32),
            pltpu.VMEM((rounds, count, width), BF16),
            pltpu.VMEM((BLOCKS, rounds, pieces, steps, envs, lane), BF16),
            pltpu.VMEM((rounds, 2, env, steps, envs, lane), BF16),
            pltpu.VMEM((rounds, steps, lane), F32),
            pltpu.VMEM((rounds, env, steps, lane), F32),
            dma((2,)),
            dma((3, BLOCKS, pieces)),
            dma((BLOCKS, LINE, 3)),
            dma((BLOCKS, env)),
            dma((BLOCKS,)),
            dma((3, rounds)),
            dma((3, rounds)),
            dma((5,)),
            dma((5,)),
            dma((BLOCKS, rounds, 2)),
            dma((BLOCKS, rounds, 2)),
            dma((BLOCKS, rounds)),
            dma((BLOCKS, rounds)),
            dma((BLOCKS, rounds, pieces)),
            dma((rounds, 2, env)),
            dma((rounds, env)),
            dma((rounds, env)),
        ],
        compiler_params=pltpu.CompilerParams(
            collective_id=0, has_side_effects=True, vmem_limit_bytes=62 * MIB
        ),
    )(
        policy_weight[0],
        obs_own[0].reshape(rounds, count, model),
        obs_opp[0].reshape(rounds, count, model),
        actions[0],
        opponent_picks,
        policy_gain,
        jnp.concatenate([value_gain, value_out])[None],
        action_table,
        value_up,
    )
    out = (turned.astype(F32) * scales[:, :, None, :]).astype(BF16)
    return (out[None], val[None])


def solution(mesh):
    in_specs = (
        P("league", None, "env", None, None),
        P("league", None, "env", None, None),
        P("league", None, None, "env", None),
        P("league", None),
        P("league", "env", None),
        P("league", None),
        P(),
        P(),
        P(),
        P(),
    )
    out_specs = (P("league", None, None, "env", None), P("league", None, "env", None))
    body = fused if mesh.shape["env"] == LINE * PAIR else local
    return jax.shard_map(body, mesh=mesh, in_specs=in_specs, out_specs=out_specs, check_vma=False)
```
